32 devices in a mesh: date: 16 (over z, y, core), strip: 2 (over x).
Axes of the slice: x: 2, y: 2, z: 4, core: 2. Of those that a mesh axis runs over, the one named last changes fastest.
Arguments:
- acquisitions: bfloat16 [32, 2, 2, 344, 640], P('date', None, None, None, 'strip'), may hold values from -6 to 6
- shifts: int32 [2, 32, 2, 5, 10], P(None, 'date', None, None, 'strip'), may hold values from -8 to 8, as said below
- fractions: int32 [2, 32, 2, 5, 10], P(None, 'date', None, None, 'strip'), may hold values from 0 to 63
- ref_dates: int32 [2], replicated, may hold values from 0 to 31, as said below
Outputs:
- chip_corr: float32 [2, 32, 2, 5, 10], P(None, 'date', None, None, 'strip')
- coherence: float32 [2, 31, 2, 64, 32], P(None, None, None, 'date', 'strip')
The draws below stay inside these ranges and needn't reach their ends.
Inputs may be any that keep to these rules, and one draw needn't show every extreme that they name: `shifts`: zero at every chip of date ref_dates[t] in tile t. `ref_dates`: the reference dates of consecutive tiles lie in different blocks of 2 dates.
All inputs are finite; a program needn't handle non-finite values.
Results may differ from the reference program's by a relative error of at most 0.0021.
Values may be sent and summed in bfloat16 or wider, within the bound.
A program may use at most 64 MiB of HBM per device.

```python
import jax
import jax.numpy as jnp
from jax import lax

DATE_DEV = 2
TILE_COUNT = 2
TILE_ROWS = 320
CHIP_SIZE = 64
MAX_SHIFT = 8
TAP_COUNT = 8
SUBSTEPS = 64
LOOK_AZ = 5
LOOK_RG = 20
DATE_COUNT = 32
TILE_COLS = 640
MARGIN = 12
CHIPS_AZ = 5
CHIPS_RG = 10
PAIR_COUNT = 31


def draw_layout(key):
    keys = jax.random.split(jax.random.fold_in(key, 11), 6)
    device_count = DATE_COUNT // DATE_DEV
    first_owner = jax.random.randint(keys[0], (), 0, device_count)
    stride = jax.random.randint(keys[1], (), 1, device_count)
    end_tile = jax.random.randint(keys[5], (), 0, TILE_COUNT)
    tile_axis = jnp.arange(TILE_COUNT, dtype=jnp.int32)
    base_owners = (first_owner + tile_axis * stride) % device_count
    owners = (base_owners - base_owners[end_tile] + device_count - 1) % device_count
    slot_pick = jax.random.randint(keys[2], (TILE_COUNT,), 0, DATE_DEV)
    slot_pick = jnp.where(tile_axis == end_tile, DATE_DEV - 1, slot_pick)
    ref_dates = (owners * DATE_DEV + slot_pick).astype(jnp.int32)
    baseline = jax.random.randint(keys[3], (2, DATE_COUNT, TILE_COUNT, 1, 1), 2 - MAX_SHIFT, MAX_SHIFT - 1)
    jitter = jax.random.randint(keys[4], (2, DATE_COUNT, TILE_COUNT, CHIPS_AZ, CHIPS_RG), -2, 3)
    is_reference = jnp.arange(DATE_COUNT, dtype=jnp.int32)[:, None] == ref_dates[None, :]
    shifts = jnp.where(is_reference[None, :, :, None, None], 0, baseline + jitter)
    return (ref_dates, shifts.astype(jnp.int32))


def draw_ref_dates(key, part):
    return draw_layout(key)[0]


def draw_shifts(key, part):
    return draw_layout(key)[1]


def draw_acquisitions(key, part):
    ref_dates, shifts = draw_layout(key)
    scene_key, noise_key = jax.random.split(jax.random.fold_in(key, 23))
    scene_shape = (TILE_COUNT, 2, TILE_ROWS + 2 * MARGIN + 2 * MAX_SHIFT, TILE_COLS + 2 * MAX_SHIFT)
    scene = jax.random.normal(scene_key, scene_shape, jnp.float32)
    line_rows = jnp.arange(TILE_ROWS + 2 * MARGIN, dtype=jnp.int32)
    line_cols = jnp.arange(TILE_COLS, dtype=jnp.int32)
    chip_rows = jnp.clip((line_rows - MARGIN) // CHIP_SIZE, 0, CHIPS_AZ - 1)
    chip_cols = line_cols // CHIP_SIZE
    tile_axis = jnp.arange(TILE_COUNT, dtype=jnp.int32)[:, None, None, None]
    part_axis = jnp.arange(2, dtype=jnp.int32)[None, :, None, None]

    def one_date(date_index):
        offsets = -lax.dynamic_index_in_dim(shifts, date_index, 1, keepdims=False)
        row_offsets = offsets[0][:, chip_rows[:, None], chip_cols[None, :]]
        col_offsets = offsets[1][:, chip_rows[:, None], chip_cols[None, :]]
        source_rows = line_rows[None, :, None] + row_offsets + MAX_SHIFT
        source_cols = line_cols[None, None, :] + col_offsets + MAX_SHIFT
        values = scene[tile_axis, part_axis, source_rows[:, None], source_cols[:, None]]
        date_key = jax.random.fold_in(noise_key, date_index)
        noise = 0.5 * jax.random.normal(date_key, values.shape, jnp.float32)
        return jnp.clip(values + noise, -6.0, 6.0)
    return lax.map(one_date, jnp.arange(DATE_COUNT, dtype=jnp.int32)).astype(jnp.bfloat16)


def touch_ends(drawn, rng, low, top_value):
    longest = drawn.shape.index(max(drawn.shape))
    spots = []
    for shift in (0, 1):
        where = [jax.random.randint(jax.random.fold_in(rng, axis), (), 0, length) for axis, length in enumerate(drawn.shape)]
        where[longest] = (where[longest] + shift) % drawn.shape[longest]
        spots.append(tuple(where))
    return drawn.at[spots[0]].set(low).at[spots[1]].set(top_value)


def setup_inputs(seed: int = 0) -> dict:
    streams_of = jax.random.split(jax.random.key(seed), 5)
    return {
        "acquisitions": draw_acquisitions(jax.random.fold_in(streams_of[4], 71), 0),
        "shifts": draw_shifts(jax.random.fold_in(streams_of[4], 71), 0),
        "fractions": touch_ends(jax.random.randint(streams_of[2], (2, DATE_COUNT, TILE_COUNT, CHIPS_AZ, CHIPS_RG), 0, SUBSTEPS), jax.random.fold_in(streams_of[2], 1), 0, SUBSTEPS - 1).astype(jnp.int32),
        "ref_dates": draw_ref_dates(jax.random.fold_in(streams_of[4], 71), 0),
    }


epsilon = 1e-06

def sinc_matrix(shift_part, fraction_part):
    window_size = CHIP_SIZE + 2 * MARGIN
    offset = fraction_part.astype(jnp.float32) / SUBSTEPS
    tap_axis = jnp.arange(TAP_COUNT).astype(jnp.float32)
    distance = tap_axis - (TAP_COUNT // 2 - 1) - offset[..., None]
    weights = jnp.sinc(distance) * (0.5 + 0.5 * jnp.cos(jnp.pi * distance / (TAP_COUNT // 2)))
    weights = weights / lax.optimization_barrier(jnp.sum(weights, axis=-1, keepdims=True))
    out_rows = jnp.arange(CHIP_SIZE, dtype=jnp.int32)[:, None]
    in_rows = jnp.arange(window_size, dtype=jnp.int32)[None, :]
    matrix = jnp.zeros(shift_part.shape + (CHIP_SIZE, window_size), jnp.float32)
    for tap_index in range(TAP_COUNT):
        target = out_rows + shift_part[..., None, None] + (tap_index - TAP_COUNT // 2 + 1 + MARGIN)
        matrix = matrix + jnp.where(in_rows == target, weights[..., tap_index][..., None, None], 0.0)
    return matrix.astype(jnp.bfloat16)

def correlate(reference_tiles, resampled):
    chips_az = resampled.shape[-2] // CHIP_SIZE
    chips_rg = resampled.shape[-1] // CHIP_SIZE

    def as_chips(values):
        return values.astype(jnp.float32).reshape(values.shape[:-2] + (chips_az, CHIP_SIZE, chips_rg, CHIP_SIZE))
    ref_chips = as_chips(reference_tiles)
    sec_chips = as_chips(resampled)
    ref_real = ref_chips[..., 0, :, :, :, :]
    ref_imag = ref_chips[..., 1, :, :, :, :]
    sec_real = sec_chips[..., 0, :, :, :, :]
    sec_imag = sec_chips[..., 1, :, :, :, :]
    cross_real = lax.optimization_barrier(jnp.sum(ref_real * sec_real + ref_imag * sec_imag, axis=(-3, -1)))
    cross_imag = lax.optimization_barrier(jnp.sum(ref_imag * sec_real - ref_real * sec_imag, axis=(-3, -1)))
    ref_power = lax.optimization_barrier(jnp.sum(ref_real * ref_real + ref_imag * ref_imag, axis=(-3, -1)))
    sec_power = lax.optimization_barrier(jnp.sum(sec_real * sec_real + sec_imag * sec_imag, axis=(-3, -1)))
    denominator = jnp.sqrt((ref_power + epsilon) * (sec_power + epsilon))
    return jnp.stack([cross_real / denominator, cross_imag / denominator])

def multilook_pairs(series):
    values = series.astype(jnp.float32)
    earlier = values[:-1]
    second = values[1:]
    early_real = earlier[:, :, 0]
    early_imag = earlier[:, :, 1]
    later_real = second[:, :, 0]
    later_imag = second[:, :, 1]
    cross_real = early_real * later_real + early_imag * later_imag
    cross_imag = early_imag * later_real - early_real * later_imag
    power_early = early_real * early_real + early_imag * early_imag
    power_later = later_real * later_real + later_imag * later_imag

    def box_sum(quantity):
        blocked = quantity.reshape(quantity.shape[:2] + (quantity.shape[2] // LOOK_AZ, LOOK_AZ, quantity.shape[3] // LOOK_RG, LOOK_RG))
        return lax.optimization_barrier(jnp.sum(blocked, axis=(3, 5)))
    denominator = jnp.sqrt((box_sum(power_early) + epsilon) * (box_sum(power_later) + epsilon))
    return jnp.stack([box_sum(cross_real) / denominator, box_sum(cross_imag) / denominator])

def reference(acquisitions, shifts, fractions, ref_dates):
    window_size = CHIP_SIZE + 2 * MARGIN
    padded = jnp.pad(acquisitions, ((0, 0), (0, 0), (0, 0), (0, 0), (MARGIN, MARGIN)))
    reference_tiles = jnp.stack([lax.dynamic_index_in_dim(acquisitions[:, tile_index], ref_dates[tile_index], 0, keepdims=False)[:, MARGIN:MARGIN + TILE_ROWS, :] for tile_index in range(TILE_COUNT)])
    row_index = (jnp.arange(CHIPS_AZ, dtype=jnp.int32) * CHIP_SIZE)[:, None] + jnp.arange(window_size, dtype=jnp.int32)[None, :]
    col_index = (jnp.arange(CHIPS_RG, dtype=jnp.int32) * CHIP_SIZE)[:, None] + jnp.arange(window_size, dtype=jnp.int32)[None, :]

    def one_date(date_index):
        date_frame = lax.dynamic_index_in_dim(padded, date_index, 0, keepdims=False)
        windows = date_frame[:, :, row_index[:, :, None, None], col_index[None, None, :, :]]
        windows = windows.transpose(0, 2, 4, 1, 3, 5).astype(jnp.float32)
        shift_now = lax.dynamic_index_in_dim(shifts, date_index, 1, keepdims=False)
        fraction_now = lax.dynamic_index_in_dim(fractions, date_index, 1, keepdims=False)
        azimuth = sinc_matrix(shift_now[0], fraction_now[0]).astype(jnp.float32)
        across = sinc_matrix(shift_now[1], fraction_now[1]).astype(jnp.float32)
        partial_rows = jnp.einsum('tariw,tarcwv->tarciv', azimuth, windows).astype(jnp.bfloat16)
        chips_out = jnp.einsum('tarciv,tarjv->tarcij', partial_rows.astype(jnp.float32), across).astype(jnp.bfloat16)
        resampled = chips_out.transpose(0, 3, 1, 4, 2, 5).reshape(TILE_COUNT, 2, TILE_ROWS, TILE_COLS)
        return (resampled, correlate(reference_tiles, resampled))
    resampled_all, corr_all = lax.map(one_date, jnp.arange(DATE_COUNT, dtype=jnp.int32))
    chip_corr = corr_all.transpose(1, 0, 2, 3, 4)

    def one_pair(pair_index):
        couple = lax.dynamic_slice_in_dim(resampled_all, pair_index, 2, 0)
        return multilook_pairs(couple)[:, 0]
    looked = lax.map(one_pair, jnp.arange(PAIR_COUNT, dtype=jnp.int32))
    coherence = looked.transpose(1, 0, 2, 3, 4)
    return (chip_corr, coherence)
```

```python
import functools

import jax
import jax.numpy as jnp
from jax import lax
from jax.experimental import pallas as pl
from jax.experimental.pallas import tpu as pltpu
from jax.sharding import PartitionSpec as P

TILE_COUNT = 2
CHIP_SIZE = 64
TAP_COUNT = 8
SUBSTEPS = 64
LOOK_AZ = 5
LOOK_RG = 20
MARGIN = 12
LANES = 128
GROUP = 8

epsilon = 1e-06
MESH = pl.DeviceIdType.MESH


def halo(block, width, dim):
    count = lax.axis_size("strip")
    forward = [(i, i + 1) for i in range(count - 1)]
    backward = [(target, source) for source, target in forward]
    low = lax.ppermute(
        lax.slice_in_dim(block, block.shape[dim] - width, None, axis=dim), "strip", forward
    )
    high = lax.ppermute(lax.slice_in_dim(block, 0, width, axis=dim), "strip", backward)
    return low, high


def tap_weights(fraction_part):
    offset = fraction_part.astype(jnp.float32) / SUBSTEPS
    tap_axis = jnp.arange(TAP_COUNT).astype(jnp.float32)
    distance = tap_axis - (TAP_COUNT // 2 - 1) - offset[..., None]
    weights = jnp.sinc(distance) * (0.5 + 0.5 * jnp.cos(jnp.pi * distance / (TAP_COUNT // 2)))
    return weights / jnp.sum(weights, axis=-1, keepdims=True)


def tap_vectors(shifts, fractions):
    weights = tap_weights(fractions)
    first = shifts + (MARGIN - TAP_COUNT // 2 + 1)
    base = (jnp.arange(shifts.shape[-1], dtype=jnp.int32) % 2) * CHIP_SIZE
    lane = jnp.arange(LANES, dtype=jnp.int32)
    lines = jnp.zeros(shifts.shape[1:] + (LANES,), jnp.float32)
    columns = lines
    for k in range(TAP_COUNT):
        lines = lines + jnp.where(
            lane == (first[0] + k)[..., None], weights[0, ..., k][..., None], 0.0
        )
        columns = columns + jnp.where(
            lane == ((base - first[1] - k) % LANES)[..., None],
            weights[1, ..., k][..., None],
            0.0,
        )
    return lines, columns


def spread_rows(row, count):
    tall = jnp.broadcast_to(row, (count, LANES))
    return pltpu.roll(tall, 0, 1, stride=1, stride_axis=0)


def split_dot(values, selector):
    high = values.astype(jnp.bfloat16)
    low = (values - high.astype(jnp.float32)).astype(jnp.bfloat16)
    return jnp.dot(high, selector, preferred_element_type=jnp.float32) + jnp.dot(
        low, selector, preferred_element_type=jnp.float32
    )


def kernel(
    n, dims,
    even_ref, odd_ref, lines_ref, cols_ref, cand_ref,
    coh_ref, sums_ref,
    series, sent, got, acc, part_buf, whole, looks, chip_rows, out_buf,
    ref_send, ref_recv, next_send, next_recv, coh_send, coh_recv,
):
    tiles, chips_az, chips_rg, rows, cols = dims
    me = lax.axis_index("date")
    bits = n.bit_length() - 1
    groups = cand_ref.shape[0]
    blocks = series.shape[3]
    wide = blocks * LANES
    bf16 = jnp.bfloat16
    f32 = jnp.float32

    barrier = pltpu.get_barrier_semaphore()
    for o in range(1, n):
        pl.semaphore_signal(
            barrier, inc=1, device_id={"date": lax.rem(me + o, n)}, device_id_type=MESH
        )
    pl.semaphore_wait(barrier, n - 1)

    offsets = [jnp.int32(0)]
    for b in range(bits):
        offsets.append(offsets[-1] + ((me // (1 << b)) % 2) * (groups >> (b + 1)))

    def partner(b):
        return me + (1 - 2 * ((me // (1 << b)) % 2)) * (1 << b)

    def halving(b):
        half = groups >> (b + 1)
        away = offsets[b] + (1 - (me // (1 << b)) % 2) * half
        source = cand_ref if b == 0 else acc
        return pltpu.make_async_remote_copy(
            src_ref=source.at[pl.ds(away, half)],
            dst_ref=part_buf.at[pl.ds(groups - 2 * half, half)],
            send_sem=ref_send.at[b],
            recv_sem=ref_recv.at[b],
            device_id={"date": partner(b)},
            device_id_type=MESH,
        )

    def add_half(b):
        half = groups >> (b + 1)
        source = cand_ref if b == 0 else acc
        target = whole if b == bits - 1 else acc

        def body(i, carry):
            g = offsets[b + 1] + i
            target[g] = source[g] + part_buf[groups - 2 * half + i]
            return carry

        lax.fori_loop(0, half, body, 0)

    def doubling(b):
        half = groups >> (b + 1)
        mine = whole.at[pl.ds(offsets[b + 1], half)]
        return pltpu.make_async_remote_copy(
            src_ref=mine,
            dst_ref=mine,
            send_sem=ref_send.at[bits + b],
            recv_sem=ref_recv.at[bits + b],
            device_id={"date": partner(b)},
            device_id_type=MESH,
        )

    state = {"step": 0, "copy": None}

    def advance():
        step = state["step"]
        if step > 2 * bits:
            return
        if step > 0:
            state["copy"].wait()
            if step <= bits:
                add_half(step - 1)
        if step < bits:
            state["copy"] = halving(step)
            state["copy"].start()
        elif step < 2 * bits:
            state["copy"] = doubling(2 * bits - 1 - step)
            state["copy"].start()
        state["step"] = step + 1

    lane = lax.broadcasted_iota(jnp.int32, (LANES, LANES), 1)
    window = 96

    def resample(d, t, first, last):
        def chip_line(a, carry):
            row0 = pl.multiple_of(a * CHIP_SIZE, CHIP_SIZE)
            q = (d * tiles + t) * 2
            for m in range((chips_rg + 1) // 2):
                span = slice(m * LANES, (m + 1) * LANES)
                halves = []
                mats = []
                for side, src in ((0, even_ref), (1, odd_ref)):
                    r = 2 * m + side
                    if r >= chips_rg:
                        continue
                    line_row = lines_ref[d * tiles + t, a, r : r + 1, :]
                    col_row = cols_ref[d * tiles + t, a, r : r + 1, :]
                    line_mat = spread_rows(line_row, CHIP_SIZE).astype(bf16)[:, :window]
                    col_mat = spread_rows(col_row, LANES)
                    keep = lane < CHIP_SIZE if side == 0 else lane >= CHIP_SIZE
                    mats.append(jnp.where(keep, col_mat, 0.0).astype(bf16))
                    both = jnp.concatenate(
                        [src[q, pl.ds(row0, window), span], src[q + 1, pl.ds(row0, window), span]],
                        axis=1,
                    )
                    halves.append(
                        jnp.dot(line_mat, both, preferred_element_type=f32).astype(bf16)
                    )
                re = jnp.concatenate([h[:, :LANES] for h in halves], axis=1)
                im = jnp.concatenate([h[:, LANES:] for h in halves], axis=1)
                stacked = jnp.concatenate([re, im], axis=0)
                matrix = jnp.concatenate(mats, axis=0)
                out = jnp.dot(stacked, matrix, preferred_element_type=f32).astype(bf16)
                for c in range(2):
                    piece = out[c * CHIP_SIZE : (c + 1) * CHIP_SIZE]
                    series[d, t, c, m, pl.ds(row0, CHIP_SIZE), :] = piece.astype(f32)
                    if d == 0:
                        sent[t, c, m, pl.ds(row0, CHIP_SIZE), :] = piece
            return carry

        lax.fori_loop(first, last, chip_line, 0)

    advance()
    middle = (chips_az + 1) // 2
    last_d = series.shape[0] - 2
    following = [None]
    for d in range(last_d + 1):
        for t in range(tiles):
            resample(d, t, 0, middle)
            advance()
            resample(d, t, middle, chips_az)
            if d == 0 and t == tiles - 1:
                following[0] = pltpu.make_async_remote_copy(
                    src_ref=sent, dst_ref=got, send_sem=next_send, recv_sem=next_recv,
                    device_id={"date": lax.rem(me + n - 1, n)}, device_id_type=MESH,
                )

                @pl.when(me > 0)
                def _():
                    following[0].start()

    @pl.when(me < n - 1)
    def _():
        following[0].wait_recv()

        def body(i, carry):
            row = pl.multiple_of(i * 16, 16)
            for t in range(tiles):
                for c in range(2):
                    for m in range(blocks):
                        series[last_d + 1, t, c, m, pl.ds(row, 16), :] = got[
                            t, c, m, pl.ds(row, 16), :
                        ].astype(f32)
            return carry

        lax.fori_loop(0, rows // 16, body, 0)

    @pl.when(me == n - 1)
    def _():
        series[last_d + 1] = jnp.zeros(series.shape[1:], f32)

    advance()
    dates = series.shape[0]
    pairs = dates - 1
    look_rows = rows // LOOK_AZ
    for t in range(tiles):
        def look_block(y, carry):
            def add(total, value):
                return value if total is None else total + value

            row = pl.multiple_of(y * GROUP, GROUP)
            for m in range(blocks):
                span = slice(m * LANES, (m + 1) * LANES)
                power = [None] * dates
                cross = [[None, None] for _ in range(pairs)]
                for s in range(LOOK_AZ):
                    lines_at = pl.ds(y * (GROUP * LOOK_AZ) + s, GROUP, stride=LOOK_AZ)
                    here = [
                        [series[d, t, c, m, lines_at, :] for c in range(2)] for d in range(dates)
                    ]
                    for d in range(dates):
                        re, im = here[d]
                        power[d] = add(power[d], re * re + im * im)
                    for p in range(pairs):
                        ar, ai = here[p]
                        br, bi = here[p + 1]
                        cross[p][0] = add(cross[p][0], ar * br + ai * bi)
                        cross[p][1] = add(cross[p][1], ai * br - ar * bi)
                for d in range(dates):
                    looks[t, d, pl.ds(row, GROUP), span] = power[d]
                for p in range(pairs):
                    for c in range(2):
                        looks[t, dates + 2 * p + c, pl.ds(row, GROUP), span] = cross[p][c]
            return carry

        lax.fori_loop(0, look_rows // GROUP, look_block, 0)
        advance()

    looks_rg = cols // LOOK_RG
    col_id = lax.broadcasted_iota(jnp.int32, (wide, LANES), 0)
    lane_id = lax.broadcasted_iota(jnp.int32, (wide, LANES), 1)
    base = col_id - LOOK_RG * lane_id

    def selector(q):
        shifted = base + LOOK_RG * looks_rg * q
        hit = (shifted >= 0) & (shifted < LOOK_RG) & (col_id < cols)
        return jnp.where(hit, 1.0, 0.0).astype(f32)

    numer = jnp.zeros((look_rows, LANES), f32)
    early = jnp.zeros((look_rows, LANES), f32)
    later = jnp.zeros((look_rows, LANES), f32)
    for p in range(pairs):
        for t in range(tiles):
            picks = [selector((c * pairs + p) * tiles + t) for c in range(2)]
            for c in range(2):
                numer = numer + split_dot(looks[t, dates + 2 * p + c], picks[c].astype(bf16))
            pick = (picks[0] + picks[1]).astype(bf16)
            early = early + split_dot(looks[t, p], pick)
            later = later + split_dot(looks[t, p + 1], pick)
    coherence = numer / jnp.sqrt((early + epsilon) * (later + epsilon))
    share = look_rows // n
    for j in range(n):
        out_buf[j] = coherence[j * share : (j + 1) * share]
    coh_ref[me] = out_buf[me]
    copies = []
    for o in range(1, n):
        peer = lax.rem(me + o, n)
        copy = pltpu.make_async_remote_copy(
            src_ref=out_buf.at[peer], dst_ref=coh_ref.at[me],
            send_sem=coh_send.at[o], recv_sem=coh_recv.at[o],
            device_id={"date": peer}, device_id_type=MESH,
        )
        copy.start()
        copies.append(copy)
    while state["step"] <= 2 * bits:
        advance()

    line_groups = CHIP_SIZE // GROUP
    kept = dates - 1
    for t in range(tiles):
        def corr_line(a, carry):
            for m in range(blocks):
                low = m * LANES
                size = min(LANES, cols - low)
                span = slice(low, low + size)
                total = [jnp.zeros((GROUP, size), f32)] * (1 + 3 * kept)
                for g in range(line_groups):
                    at = a * line_groups + g
                    rr = whole[(t * 2) * (rows // GROUP) + at, :, span].astype(f32)
                    ri = whole[(t * 2 + 1) * (rows // GROUP) + at, :, span].astype(f32)
                    total[0] = total[0] + (rr * rr + ri * ri)
                    row = pl.multiple_of(at * GROUP, GROUP)
                    for d in range(kept):
                        sr = series[d, t, 0, m, pl.ds(row, GROUP), :size]
                        si = series[d, t, 1, m, pl.ds(row, GROUP), :size]
                        total[1 + 3 * d] = total[1 + 3 * d] + (rr * sr + ri * si)
                        total[2 + 3 * d] = total[2 + 3 * d] + (ri * sr - rr * si)
                        total[3 + 3 * d] = total[3 + 3 * d] + (sr * sr + si * si)
                for k in range(1 + 3 * kept):
                    chip_rows[t, a, k : k + 1, span] = jnp.sum(total[k], axis=0, keepdims=True)
            return carry

        lax.fori_loop(0, chips_az, corr_line, 0)
    col_id = lax.broadcasted_iota(jnp.int32, (cols, LANES), 0)
    lane_id = lax.broadcasted_iota(jnp.int32, (cols, LANES), 1)
    gap = col_id - CHIP_SIZE * lane_id
    pick = jnp.where((gap >= 0) & (gap < CHIP_SIZE), 1.0, 0.0).astype(bf16)
    for t in range(tiles):
        for a in range(chips_az):
            sums_ref[t, a] = split_dot(chip_rows[t, a], pick)

    for o in range(1, n):
        copies[o - 1].wait()

    @pl.when(me > 0)
    def _():
        following[0].wait_send()


def per_device(n, acquisitions, shifts, fractions, ref_dates):
    dates_local, tiles, _, all_rows, cols = acquisitions.shape
    rows = all_rows - 2 * MARGIN
    chips_az, chips_rg = shifts.shape[3:]
    wide = -(-cols // LANES) * LANES
    low, high = halo(acquisitions, MARGIN, 4)
    owners = ref_dates // dates_local
    slots = ref_dates % dates_local
    me = lax.axis_index("date")
    cand = jnp.stack(
        [
            jnp.where(
                owners[t] == me,
                lax.dynamic_index_in_dim(acquisitions[:, t], slots[t], 0, keepdims=False)[
                    :, MARGIN : MARGIN + rows, :
                ],
                0,
            ).astype(acquisitions.dtype)
            for t in range(tiles)
        ]
    ).reshape(tiles * 2 * rows // GROUP, GROUP, cols)
    padded = jnp.concatenate([low, acquisitions, high], axis=4)
    flat = padded.reshape((-1,) + padded.shape[3:])
    tall = -(-all_rows // 32) * 32
    even = jnp.pad(flat, ((0, 0), (0, tall - all_rows), (0, wide - flat.shape[2])))
    odd_wide = (chips_rg // 2) * LANES
    odd = even[:, :, CHIP_SIZE : CHIP_SIZE + odd_wide]
    lines, columns = tap_vectors(shifts, fractions)
    lines = lines.reshape((-1,) + lines.shape[2:])
    columns = columns.reshape((-1,) + columns.shape[2:])

    look_rows = rows // LOOK_AZ
    looks_rg = cols // LOOK_RG
    share = look_rows // n
    stat_rows = 1 + 3 * dates_local
    bits = n.bit_length() - 1
    vmem = pl.BlockSpec(memory_space=pltpu.VMEM)
    f32 = jnp.float32
    bf16 = jnp.bfloat16
    groups = cand.shape[0]
    dma = pltpu.SemaphoreType.DMA
    coh, sums = pl.pallas_call(
        functools.partial(kernel, n, (tiles, chips_az, chips_rg, rows, cols)),
        out_shape=(
            jax.ShapeDtypeStruct((n, share, LANES), f32),
            jax.ShapeDtypeStruct((tiles, chips_az, stat_rows, LANES), f32),
        ),
        in_specs=[vmem] * 5,
        out_specs=(vmem, vmem),
        scratch_shapes=[
            pltpu.VMEM((dates_local + 1, tiles, 2, wide // LANES, rows, LANES), f32),
            pltpu.VMEM((tiles, 2, wide // LANES, rows, LANES), bf16),
            pltpu.VMEM((tiles, 2, wide // LANES, rows, LANES), bf16),
            pltpu.VMEM((groups, GROUP, cols), bf16),
            pltpu.VMEM((groups, GROUP, cols), bf16),
            pltpu.VMEM((groups, GROUP, cols), bf16),
            pltpu.VMEM((tiles, dates_local + 1 + 2 * dates_local, look_rows, wide), f32),
            pltpu.VMEM((tiles, chips_az, stat_rows, cols), f32),
            pltpu.VMEM((n, share, LANES), f32),
            dma((2 * bits,)), dma((2 * bits,)), dma, dma, dma((n,)), dma((n,)),
        ],
        compiler_params=pltpu.CompilerParams(
            collective_id=0, has_side_effects=True, vmem_limit_bytes=50 * 1024 * 1024
        ),
    )(even, odd, lines, columns, cand)

    stats = sums[..., :chips_rg]
    ref_power = stats[:, :, 0]
    sec = stats[:, :, 1:].reshape(tiles, chips_az, dates_local, 3, chips_rg)
    sec = sec.transpose(3, 2, 0, 1, 4)
    denominator = jnp.sqrt((ref_power[None] + epsilon) * (sec[2] + epsilon))
    chip_corr = sec[:2] / denominator[None]
    looked = coh.reshape(n, share, 2, dates_local, tiles, looks_rg)
    looked = looked.transpose(2, 0, 3, 4, 1, 5).reshape(2, n * dates_local, tiles, share, looks_rg)
    return (chip_corr, looked[:, : n * dates_local - 1])


def solution(mesh):
    return jax.shard_map(
        functools.partial(per_device, mesh.shape["date"]),
        mesh=mesh,
        in_specs=(
            P("date", None, None, None, "strip"),
            P(None, "date", None, None, "strip"),
            P(None, "date", None, None, "strip"),
            P(),
        ),
        out_specs=(P(None, "date", None, None, "strip"), P(None, None, None, "date", "strip")),
        check_vma=False,
    )
```

```python
import functools

import jax
import jax.numpy as jnp
from jax import lax
from jax.experimental import pallas as pl
from jax.experimental.pallas import tpu as pltpu
from jax.sharding import PartitionSpec as P

TILE_COUNT = 2
CHIP_SIZE = 64
TAP_COUNT = 8
SUBSTEPS = 64
LOOK_AZ = 5
LOOK_RG = 20
MARGIN = 12
LANES = 128
GROUP = 8

epsilon = 1e-06
MESH = pl.DeviceIdType.MESH


def tap_weights(k, fraction):
    distance = k.astype(jnp.float32) - (TAP_COUNT // 2 - 1) - fraction.astype(jnp.float32) / SUBSTEPS
    angle = jnp.pi * distance
    sinc = jnp.where(
        distance == 0.0, 1.0, jnp.sin(angle) / jnp.where(distance == 0.0, 1.0, angle)
    )
    weights = sinc * (0.5 + 0.5 * jnp.cos(jnp.pi * distance / (TAP_COUNT // 2)))
    weights = jnp.where((k >= 0) & (k < TAP_COUNT), weights, 0.0)
    return weights / jnp.sum(weights, axis=1, keepdims=True)


def spread_rows(row, count):
    tall = jnp.broadcast_to(row, (count, LANES))
    return pltpu.roll(tall, 0, 1, stride=1, stride_axis=0)


def split_dot(values, selector):
    high = values.astype(jnp.bfloat16)
    low = (values - high.astype(jnp.float32)).astype(jnp.bfloat16)
    return jnp.dot(high, selector, preferred_element_type=jnp.float32) + jnp.dot(
        low, selector, preferred_element_type=jnp.float32
    )


def kernel(
    n, strips, dims,
    frame_ref, shifts_ref, fractions_ref, dates_ref,
    coh_ref, sums_ref,
    even_ref, odd_ref, lines_ref, cols_ref, cand_ref, edge_out, edge_in, picked, spots,
    series, sent, got, acc, part_buf, whole, looks, chip_rows, out_buf,
    ref_send, ref_recv, next_send, next_recv, coh_send, coh_recv, edge_send, edge_recv,
):
    tiles, chips_az, chips_rg, rows, cols = dims
    me = lax.axis_index("date")
    strip = lax.axis_index("strip")
    bits = n.bit_length() - 1
    groups = cand_ref.shape[0]
    all_rows = rows + 2 * MARGIN
    blocks = series.shape[3]
    wide = blocks * LANES
    kept_dates = series.shape[0] - 1
    images = frame_ref.shape[0]
    rest = cols - (blocks - 1) * LANES
    bf16 = jnp.bfloat16
    f32 = jnp.float32

    barrier = pltpu.get_barrier_semaphore()
    for o in range(1, n):
        pl.semaphore_signal(
            barrier, inc=1, device_id={"date": lax.rem(me + o, n)}, device_id_type=MESH
        )
    has_low = strip > 0
    has_high = strip < strips - 1

    @pl.when(has_low)
    def _():
        pl.semaphore_signal(barrier, inc=1, device_id={"strip": strip - 1}, device_id_type=MESH)

    @pl.when(has_high)
    def _():
        pl.semaphore_signal(barrier, inc=1, device_id={"strip": strip + 1}, device_id_type=MESH)

    def for_rows(body):
        count = all_rows // CHIP_SIZE

        def step(i, carry):
            body(pl.multiple_of(i * CHIP_SIZE, CHIP_SIZE), CHIP_SIZE)
            return carry

        lax.fori_loop(0, count, step, 0)
        if all_rows > count * CHIP_SIZE:
            body(count * CHIP_SIZE, all_rows - count * CHIP_SIZE)

    def block_of(q, row, size, m):
        width = min(LANES, cols - m * LANES)
        value = frame_ref[q, pl.ds(row, size), m * LANES : m * LANES + width].astype(f32)
        if width < LANES:
            value = jnp.concatenate([value, jnp.zeros((size, LANES - width), f32)], axis=1)
        return value

    def pack_edges(row, size):
        at = lax.broadcasted_iota(jnp.int32, (size, LANES), 1)
        right = jnp.zeros((size, LANES), f32)
        left = jnp.zeros((size, LANES), f32)
        for q in range(images):
            place = (at >= MARGIN * q) & (at < MARGIN * (q + 1))
            last = block_of(q, row, size, blocks - 1)
            first = block_of(q, row, size, 0)
            last = pltpu.roll(last, (MARGIN * q - rest + MARGIN) % LANES, 1)
            if q:
                first = pltpu.roll(first, MARGIN * q, 1)
            right = jnp.where(place, last, right)
            left = jnp.where(place, first, left)
        edge_out[0, pl.ds(row, size), :] = right.astype(bf16)
        edge_out[1, pl.ds(row, size), :] = left.astype(bf16)

    for_rows(pack_edges)

    def pick_tile(tc, carry):
        t = tc // 2
        gains = [
            jnp.where(dates_ref[t] == me * kept_dates + d, 1.0, 0.0).astype(f32)
            for d in range(kept_dates)
        ]

        def select(row, size):
            total = jnp.zeros((size, cols), f32)
            for d in range(kept_dates):
                image = frame_ref[d * tiles * 2 + tc, pl.ds(row, size), :]
                total = total + image.astype(f32) * gains[d]
            picked[pl.ds(row, size), :] = total

        for_rows(select)
        count = rows // GROUP
        for g in range(count):
            low = MARGIN + g * GROUP
            cand_ref[tc * count + g] = picked[low : low + GROUP, :].astype(bf16)
        return carry

    lax.fori_loop(0, tiles * 2, pick_tile, 0)

    beside = jnp.minimum(strip, 1) + jnp.minimum(strips - 1 - strip, 1)
    pl.semaphore_wait(barrier, n - 1 + beside)

    edges = [
        pltpu.make_async_remote_copy(
            src_ref=edge_out.at[i], dst_ref=edge_in.at[i],
            send_sem=edge_send.at[i], recv_sem=edge_recv.at[i],
            device_id={"strip": strip + 1 - 2 * i}, device_id_type=MESH,
        )
        for i in range(2)
    ]

    @pl.when(has_high)
    def _():
        edges[0].start()

    @pl.when(has_low)
    def _():
        edges[1].start()

    offsets = [jnp.int32(0)]
    for b in range(bits):
        offsets.append(offsets[-1] + ((me // (1 << b)) % 2) * (groups >> (b + 1)))

    def partner(b):
        return me + (1 - 2 * ((me // (1 << b)) % 2)) * (1 << b)

    def halving(b):
        half = groups >> (b + 1)
        away = offsets[b] + (1 - (me // (1 << b)) % 2) * half
        source = cand_ref if b == 0 else acc
        return pltpu.make_async_remote_copy(
            src_ref=source.at[pl.ds(away, half)],
            dst_ref=part_buf.at[pl.ds(groups - 2 * half, half)],
            send_sem=ref_send.at[b],
            recv_sem=ref_recv.at[b],
            device_id={"date": partner(b)},
            device_id_type=MESH,
        )

    def add_half(b):
        half = groups >> (b + 1)
        source = cand_ref if b == 0 else acc
        target = whole if b == bits - 1 else acc

        def body(i, carry):
            g = offsets[b + 1] + i
            target[g] = source[g] + part_buf[groups - 2 * half + i]
            return carry

        lax.fori_loop(0, half, body, 0)

    def doubling(b):
        half = groups >> (b + 1)
        mine = whole.at[pl.ds(offsets[b + 1], half)]
        return pltpu.make_async_remote_copy(
            src_ref=mine,
            dst_ref=mine,
            send_sem=ref_send.at[bits + b],
            recv_sem=ref_recv.at[bits + b],
            device_id={"date": partner(b)},
            device_id_type=MESH,
        )

    state = {"step": 0, "copy": None}

    def advance():
        step = state["step"]
        if step > 2 * bits:
            return
        if step > 0:
            state["copy"].wait()
            if step <= bits:
                add_half(step - 1)
        if step < bits:
            state["copy"] = halving(step)
            state["copy"].start()
        elif step < 2 * bits:
            state["copy"] = doubling(2 * bits - 1 - step)
            state["copy"].start()
        state["step"] = step + 1

    lane = lax.broadcasted_iota(jnp.int32, (LANES, LANES), 1)
    window = 96

    def resample(d, t, first, last):
        def chip_line(a, carry):
            row0 = pl.multiple_of(a * CHIP_SIZE, CHIP_SIZE)
            q = (d * tiles + t) * 2
            for m in range((chips_rg + 1) // 2):
                span = slice(m * LANES, (m + 1) * LANES)
                halves = []
                mats = []
                for side, src in ((0, even_ref), (1, odd_ref)):
                    r = 2 * m + side
                    if r >= chips_rg:
                        continue
                    row_at = ((d * tiles + t) * chips_az + a) * chips_rg + r
                    line_row = lines_ref[pl.ds(row_at, 1), :]
                    col_row = cols_ref[pl.ds(row_at, 1), :]
                    line_mat = spread_rows(line_row, CHIP_SIZE).astype(bf16)[:, :window]
                    col_mat = spread_rows(col_row, LANES)
                    keep = lane < CHIP_SIZE if side == 0 else lane >= CHIP_SIZE
                    mats.append(jnp.where(keep, col_mat, 0.0).astype(bf16))
                    both = jnp.concatenate(
                        [src[q, pl.ds(row0, window), span], src[q + 1, pl.ds(row0, window), span]],
                        axis=1,
                    )
                    halves.append(
                        jnp.dot(line_mat, both, preferred_element_type=f32).astype(bf16)
                    )
                re = jnp.concatenate([h[:, :LANES] for h in halves], axis=1)
                im = jnp.concatenate([h[:, LANES:] for h in halves], axis=1)
                stacked = jnp.concatenate([re, im], axis=0)
                matrix = jnp.concatenate(mats, axis=0)
                out = jnp.dot(stacked, matrix, preferred_element_type=f32).astype(bf16)
                for c in range(2):
                    piece = out[c * CHIP_SIZE : (c + 1) * CHIP_SIZE]
                    series[d, t, c, m, pl.ds(row0, CHIP_SIZE), :] = piece.astype(f32)
                    if d == 0:
                        sent[t, c, m, pl.ds(row0, CHIP_SIZE), :] = piece
            return carry

        lax.fori_loop(first, last, chip_line, 0)

    advance()

    chip = 0
    for d in range(kept_dates):
        for t in range(tiles):
            for a in range(chips_az):
                for r in range(chips_rg):
                    values = (
                        shifts_ref[0, d, t, a, r] + (MARGIN - TAP_COUNT // 2 + 1),
                        (r % 2) * CHIP_SIZE
                        - shifts_ref[1, d, t, a, r]
                        - (MARGIN - TAP_COUNT // 2 + 1),
                        fractions_ref[0, d, t, a, r],
                        fractions_ref[1, d, t, a, r],
                    )
                    for i, value in enumerate(values):
                        spots[i, chip : chip + 1, :] = jnp.full((1, LANES), value, jnp.int32)
                    chip += 1
    at = lax.broadcasted_iota(jnp.int32, (chip, LANES), 1)
    lines_ref[:chip] = tap_weights(at - spots[0, :chip], spots[2, :chip])
    cols_ref[:chip] = tap_weights((spots[1, :chip] - at) & (LANES - 1), spots[3, :chip])

    @pl.when(has_low)
    def _():
        edges[0].wait_recv()

    @pl.when(has_high)
    def _():
        edges[1].wait_recv()

    @pl.when(strip == 0)
    def _():
        edge_in[0] = jnp.zeros(edge_in.shape[1:], bf16)

    @pl.when(strip == strips - 1)
    def _():
        edge_in[1] = jnp.zeros(edge_in.shape[1:], bf16)

    advance()
    tall = even_ref.shape[1]

    def shift_image(q, carry):
        def body(row, size):
            at = lax.broadcasted_iota(jnp.int32, (size, LANES), 1)
            low = edge_in[0, pl.ds(row, size), :].astype(f32)
            high = edge_in[1, pl.ds(row, size), :].astype(f32)
            low = pltpu.roll(low, lax.rem(LANES - MARGIN * q, LANES), 1)
            high = pltpu.roll(high, lax.rem(2 * LANES + rest + MARGIN - MARGIN * q, LANES), 1)
            moved = [pltpu.roll(block_of(q, row, size, m), MARGIN, 1) for m in range(blocks)]
            even = [
                jnp.where(at < MARGIN, low if m == 0 else moved[m - 1], moved[m])
                for m in range(blocks)
            ]
            ends = (at >= rest + MARGIN) & (at < rest + 2 * MARGIN)
            even[-1] = jnp.where(ends, high, even[-1])
            half = [pltpu.roll(value, CHIP_SIZE, 1) for value in even]
            for m in range(blocks):
                even_ref[q, pl.ds(row, size), m * LANES : (m + 1) * LANES] = even[m].astype(bf16)
            for m in range(chips_rg // 2):
                value = jnp.where(at < CHIP_SIZE, half[m], half[m + 1])
                odd_ref[q, pl.ds(row, size), m * LANES : (m + 1) * LANES] = value.astype(bf16)

        for_rows(body)
        even_ref[q, all_rows:, :] = jnp.zeros((tall - all_rows, wide), bf16)
        odd_ref[q, all_rows:, :] = jnp.zeros((tall - all_rows, odd_ref.shape[2]), bf16)
        return carry

    lax.fori_loop(0, images, shift_image, 0)
    middle = (chips_az + 1) // 2
    last_d = series.shape[0] - 2
    following = [None]
    for d in range(last_d + 1):
        for t in range(tiles):
            resample(d, t, 0, middle)
            advance()
            resample(d, t, middle, chips_az)
            if d == 0 and t == tiles - 1:
                following[0] = pltpu.make_async_remote_copy(
                    src_ref=sent, dst_ref=got, send_sem=next_send, recv_sem=next_recv,
                    device_id={"date": lax.rem(me + n - 1, n)}, device_id_type=MESH,
                )

                @pl.when(me > 0)
                def _():
                    following[0].start()

    @pl.when(me < n - 1)
    def _():
        following[0].wait_recv()

        def body(i, carry):
            row = pl.multiple_of(i * 16, 16)
            for t in range(tiles):
                for c in range(2):
                    for m in range(blocks):
                        series[last_d + 1, t, c, m, pl.ds(row, 16), :] = got[
                            t, c, m, pl.ds(row, 16), :
                        ].astype(f32)
            return carry

        lax.fori_loop(0, rows // 16, body, 0)

    @pl.when(me == n - 1)
    def _():
        series[last_d + 1] = jnp.zeros(series.shape[1:], f32)

    advance()
    dates = series.shape[0]
    pairs = dates - 1
    look_rows = rows // LOOK_AZ
    for t in range(tiles):
        def look_block(y, carry):
            def add(total, value):
                return value if total is None else total + value

            row = pl.multiple_of(y * GROUP, GROUP)
            for m in range(blocks):
                span = slice(m * LANES, (m + 1) * LANES)
                power = [None] * dates
                cross = [[None, None] for _ in range(pairs)]
                for s in range(LOOK_AZ):
                    lines_at = pl.ds(y * (GROUP * LOOK_AZ) + s, GROUP, stride=LOOK_AZ)
                    here = [
                        [series[d, t, c, m, lines_at, :] for c in range(2)] for d in range(dates)
                    ]
                    for d in range(dates):
                        re, im = here[d]
                        power[d] = add(power[d], re * re + im * im)
                    for p in range(pairs):
                        ar, ai = here[p]
                        br, bi = here[p + 1]
                        cross[p][0] = add(cross[p][0], ar * br + ai * bi)
                        cross[p][1] = add(cross[p][1], ai * br - ar * bi)
                for d in range(dates):
                    looks[t, d, pl.ds(row, GROUP), span] = power[d]
                for p in range(pairs):
                    for c in range(2):
                        looks[t, dates + 2 * p + c, pl.ds(row, GROUP), span] = cross[p][c]
            return carry

        lax.fori_loop(0, look_rows // GROUP, look_block, 0)
        advance()

    looks_rg = cols // LOOK_RG
    col_id = lax.broadcasted_iota(jnp.int32, (wide, LANES), 0)
    lane_id = lax.broadcasted_iota(jnp.int32, (wide, LANES), 1)
    base = col_id - LOOK_RG * lane_id

    def selector(q):
        shifted = base + LOOK_RG * looks_rg * q
        hit = (shifted >= 0) & (shifted < LOOK_RG) & (col_id < cols)
        return jnp.where(hit, 1.0, 0.0).astype(f32)

    numer = jnp.zeros((look_rows, LANES), f32)
    early = jnp.zeros((look_rows, LANES), f32)
    later = jnp.zeros((look_rows, LANES), f32)
    for p in range(pairs):
        for t in range(tiles):
            picks = [selector((c * pairs + p) * tiles + t) for c in range(2)]
            for c in range(2):
                numer = numer + split_dot(looks[t, dates + 2 * p + c], picks[c].astype(bf16))
            pick = (picks[0] + picks[1]).astype(bf16)
            early = early + split_dot(looks[t, p], pick)
            later = later + split_dot(looks[t, p + 1], pick)
    coherence = numer / jnp.sqrt((early + epsilon) * (later + epsilon))
    share = look_rows // n
    for j in range(n):
        out_buf[j] = coherence[j * share : (j + 1) * share]
    coh_ref[me] = out_buf[me]
    copies = []
    for o in range(1, n):
        peer = lax.rem(me + o, n)
        copy = pltpu.make_async_remote_copy(
            src_ref=out_buf.at[peer], dst_ref=coh_ref.at[me],
            send_sem=coh_send.at[o], recv_sem=coh_recv.at[o],
            device_id={"date": peer}, device_id_type=MESH,
        )
        copy.start()
        copies.append(copy)
    while state["step"] <= 2 * bits:
        advance()

    line_groups = CHIP_SIZE // GROUP
    kept = dates - 1
    for t in range(tiles):
        def corr_line(a, carry):
            for m in range(blocks):
                low = m * LANES
                size = min(LANES, cols - low)
                span = slice(low, low + size)
                total = [jnp.zeros((GROUP, size), f32)] * (1 + 3 * kept)
                for g in range(line_groups):
                    at = a * line_groups + g
                    rr = whole[(t * 2) * (rows // GROUP) + at, :, span].astype(f32)
                    ri = whole[(t * 2 + 1) * (rows // GROUP) + at, :, span].astype(f32)
                    total[0] = total[0] + (rr * rr + ri * ri)
                    row = pl.multiple_of(at * GROUP, GROUP)
                    for d in range(kept):
                        sr = series[d, t, 0, m, pl.ds(row, GROUP), :size]
                        si = series[d, t, 1, m, pl.ds(row, GROUP), :size]
                        total[1 + 3 * d] = total[1 + 3 * d] + (rr * sr + ri * si)
                        total[2 + 3 * d] = total[2 + 3 * d] + (ri * sr - rr * si)
                        total[3 + 3 * d] = total[3 + 3 * d] + (sr * sr + si * si)
                for k in range(1 + 3 * kept):
                    chip_rows[t, a, k : k + 1, span] = jnp.sum(total[k], axis=0, keepdims=True)
            return carry

        lax.fori_loop(0, chips_az, corr_line, 0)
    col_id = lax.broadcasted_iota(jnp.int32, (cols, LANES), 0)
    lane_id = lax.broadcasted_iota(jnp.int32, (cols, LANES), 1)
    gap = col_id - CHIP_SIZE * lane_id
    pick = jnp.where((gap >= 0) & (gap < CHIP_SIZE), 1.0, 0.0).astype(bf16)
    for t in range(tiles):
        for a in range(chips_az):
            sums_ref[t, a] = split_dot(chip_rows[t, a], pick)

    for o in range(1, n):
        copies[o - 1].wait()

    @pl.when(me > 0)
    def _():
        following[0].wait_send()

    @pl.when(has_high)
    def _():
        edges[0].wait_send()

    @pl.when(has_low)
    def _():
        edges[1].wait_send()


def per_device(n, strips, acquisitions, shifts, fractions, ref_dates):
    dates_local, tiles, _, all_rows, cols = acquisitions.shape
    rows = all_rows - 2 * MARGIN
    chips_az, chips_rg = shifts.shape[3:]
    blocks = -(-cols // LANES)
    wide = blocks * LANES
    images = dates_local * tiles * 2
    frames = acquisitions.reshape(images, all_rows, cols)
    tall = -(-all_rows // 32) * 32
    odd_wide = (chips_rg // 2) * LANES
    chips = dates_local * tiles * chips_az * chips_rg
    chips_tall = -(-chips // GROUP) * GROUP
    groups = tiles * 2 * rows // GROUP

    look_rows = rows // LOOK_AZ
    looks_rg = cols // LOOK_RG
    share = look_rows // n
    stat_rows = 1 + 3 * dates_local
    bits = n.bit_length() - 1
    vmem = pl.BlockSpec(memory_space=pltpu.VMEM)
    f32 = jnp.float32
    bf16 = jnp.bfloat16
    dma = pltpu.SemaphoreType.DMA
    coh, sums = pl.pallas_call(
        functools.partial(kernel, n, strips, (tiles, chips_az, chips_rg, rows, cols)),
        out_shape=(
            jax.ShapeDtypeStruct((n, share, LANES), f32),
            jax.ShapeDtypeStruct((tiles, chips_az, stat_rows, LANES), f32),
        ),
        in_specs=[vmem] + [pl.BlockSpec(memory_space=pltpu.SMEM)] * 3,
        out_specs=(vmem, vmem),
        scratch_shapes=[
            pltpu.VMEM((images, tall, wide), bf16),
            pltpu.VMEM((images, tall, odd_wide), bf16),
            pltpu.VMEM((chips_tall, LANES), f32),
            pltpu.VMEM((chips_tall, LANES), f32),
            pltpu.VMEM((groups, GROUP, cols), bf16),
            pltpu.VMEM((2, all_rows, LANES), bf16),
            pltpu.VMEM((2, all_rows, LANES), bf16),
            pltpu.VMEM((all_rows, cols), f32),
            pltpu.VMEM((4, chips_tall, LANES), jnp.int32),
            pltpu.VMEM((dates_local + 1, tiles, 2, wide // LANES, rows, LANES), f32),
            pltpu.VMEM((tiles, 2, wide // LANES, rows, LANES), bf16),
            pltpu.VMEM((tiles, 2, wide // LANES, rows, LANES), bf16),
            pltpu.VMEM((groups, GROUP, cols), bf16),
            pltpu.VMEM((groups, GROUP, cols), bf16),
            pltpu.VMEM((groups, GROUP, cols), bf16),
            pltpu.VMEM((tiles, dates_local + 1 + 2 * dates_local, look_rows, wide), f32),
            pltpu.VMEM((tiles, chips_az, stat_rows, cols), f32),
            pltpu.VMEM((n, share, LANES), f32),
            dma((2 * bits,)), dma((2 * bits,)), dma, dma, dma((n,)), dma((n,)),
            dma((2,)), dma((2,)),
        ],
        compiler_params=pltpu.CompilerParams(
            collective_id=0, has_side_effects=True, vmem_limit_bytes=50 * 1024 * 1024
        ),
    )(frames, shifts, fractions, ref_dates)

    stats = sums[..., :chips_rg]
    ref_power = stats[:, :, 0]
    sec = stats[:, :, 1:].reshape(tiles, chips_az, dates_local, 3, chips_rg)
    sec = sec.transpose(3, 2, 0, 1, 4)
    denominator = jnp.sqrt((ref_power[None] + epsilon) * (sec[2] + epsilon))
    chip_corr = sec[:2] / denominator[None]
    looked = coh.reshape(n, share, 2, dates_local, tiles, looks_rg)
    looked = looked.transpose(2, 0, 3, 4, 1, 5).reshape(2, n * dates_local, tiles, share, looks_rg)
    return (chip_corr, looked[:, : n * dates_local - 1])


def solution(mesh):
    return jax.shard_map(
        functools.partial(per_device, mesh.shape["date"], mesh.shape["strip"]),
        mesh=mesh,
        in_specs=(
            P("date", None, None, None, "strip"),
            P(None, "date", None, None, "strip"),
            P(None, "date", None, None, "strip"),
            P(),
        ),
        out_specs=(P(None, "date", None, None, "strip"), P(None, None, None, "date", "strip")),
        check_vma=False,
    )
```

```python
import functools

import jax
import jax.numpy as jnp
from jax import lax
from jax.experimental import pallas as pl
from jax.experimental.pallas import tpu as pltpu
from jax.sharding import PartitionSpec as P

TILE_COUNT = 2
CHIP_SIZE = 64
TAP_COUNT = 8
SUBSTEPS = 64
LOOK_AZ = 5
LOOK_RG = 20
MARGIN = 12
LANES = 128
GROUP = 8

epsilon = 1e-06
MESH = pl.DeviceIdType.MESH


def tap_weights(k, fraction):
    distance = k.astype(jnp.float32) - (TAP_COUNT // 2 - 1) - fraction.astype(jnp.float32) / SUBSTEPS
    angle = jnp.pi * distance
    sinc = jnp.where(
        distance == 0.0, 1.0, jnp.sin(angle) / jnp.where(distance == 0.0, 1.0, angle)
    )
    weights = sinc * (0.5 + 0.5 * jnp.cos(jnp.pi * distance / (TAP_COUNT // 2)))
    weights = jnp.where((k >= 0) & (k < TAP_COUNT), weights, 0.0)
    return weights / jnp.sum(weights, axis=1, keepdims=True)


def spread_rows(row, count):
    tall = jnp.broadcast_to(row, (count, LANES))
    return pltpu.roll(tall, 0, 1, stride=1, stride_axis=0)


def split_dot(values, selector):
    high = values.astype(jnp.bfloat16)
    low = (values - high.astype(jnp.float32)).astype(jnp.bfloat16)
    return jnp.dot(high, selector, preferred_element_type=jnp.float32) + jnp.dot(
        low, selector, preferred_element_type=jnp.float32
    )


def kernel(
    n, strips, dims,
    frame_hbm, shifts_ref, fractions_ref, dates_ref,
    coh_ref, sums_ref,
    frame_ref, frame_sem, even_ref, odd_ref, lines_ref, cols_ref, cand_ref, edge_out, edge_in, picked, spots,
    series, sent, got, acc, part_buf, whole, looks, chip_rows, out_buf,
    ref_send, ref_recv, next_send, next_recv, coh_send, coh_recv, edge_send, edge_recv,
):
    tiles, chips_az, chips_rg, rows, cols = dims
    me = lax.axis_index("date")
    strip = lax.axis_index("strip")
    bits = n.bit_length() - 1
    groups = cand_ref.shape[1]
    all_rows = rows + 2 * MARGIN
    blocks = series.shape[3]
    wide = blocks * LANES
    kept_dates = series.shape[0] - 1
    images = frame_ref.shape[0]
    rest = cols - (blocks - 1) * LANES
    bf16 = jnp.bfloat16
    f32 = jnp.float32

    load = pltpu.make_async_copy(frame_hbm, frame_ref, frame_sem)
    load.start()
    barrier = pltpu.get_barrier_semaphore()
    for o in range(1, n):
        pl.semaphore_signal(
            barrier, inc=1, device_id={"date": lax.rem(me + o, n)}, device_id_type=MESH
        )
    has_low = strip > 0
    has_high = strip < strips - 1

    @pl.when(has_low)
    def _():
        pl.semaphore_signal(barrier, inc=1, device_id={"strip": strip - 1}, device_id_type=MESH)

    @pl.when(has_high)
    def _():
        pl.semaphore_signal(barrier, inc=1, device_id={"strip": strip + 1}, device_id_type=MESH)

    def for_rows(body):
        count = all_rows // CHIP_SIZE

        def step(i, carry):
            body(pl.multiple_of(i * CHIP_SIZE, CHIP_SIZE), CHIP_SIZE)
            return carry

        lax.fori_loop(0, count, step, 0)
        if all_rows > count * CHIP_SIZE:
            body(count * CHIP_SIZE, all_rows - count * CHIP_SIZE)

    def block_of(q, row, size, m):
        width = min(LANES, cols - m * LANES)
        value = frame_ref[q, pl.ds(row, size), m * LANES : m * LANES + width].astype(f32)
        if width < LANES:
            value = jnp.concatenate([value, jnp.zeros((size, LANES - width), f32)], axis=1)
        return value

    def pack_edges(row, size):
        at = lax.broadcasted_iota(jnp.int32, (size, LANES), 1)
        right = jnp.zeros((size, LANES), f32)
        left = jnp.zeros((size, LANES), f32)
        for q in range(images):
            place = (at >= MARGIN * q) & (at < MARGIN * (q + 1))
            last = block_of(q, row, size, blocks - 1)
            first = block_of(q, row, size, 0)
            last = pltpu.roll(last, (MARGIN * q - rest + MARGIN) % LANES, 1)
            if q:
                first = pltpu.roll(first, MARGIN * q, 1)
            right = jnp.where(place, last, right)
            left = jnp.where(place, first, left)
        edge_out[0, pl.ds(row, size), :] = right.astype(bf16)
        edge_out[1, pl.ds(row, size), :] = left.astype(bf16)

    load.wait()
    for_rows(pack_edges)

    def pick_tile(tc, carry):
        t = tc // 2
        gains = [
            jnp.where(dates_ref[t] == me * kept_dates + d, 1.0, 0.0).astype(f32)
            for d in range(kept_dates)
        ]

        def select(row, size):
            total = jnp.zeros((size, cols), f32)
            for d in range(kept_dates):
                image = frame_ref[d * tiles * 2 + tc, pl.ds(row, size), :]
                total = total + image.astype(f32) * gains[d]
            picked[pl.ds(row, size), :] = total

        for_rows(select)
        count = rows // GROUP
        for g in range(count):
            low = MARGIN + g * GROUP
            cand_ref[t, (tc % 2) * count + g] = picked[low : low + GROUP, :].astype(bf16)
        return carry

    lax.fori_loop(0, tiles * 2, pick_tile, 0)

    beside = jnp.minimum(strip, 1) + jnp.minimum(strips - 1 - strip, 1)
    pl.semaphore_wait(barrier, n - 1 + beside)

    edges = [
        pltpu.make_async_remote_copy(
            src_ref=edge_out.at[i], dst_ref=edge_in.at[i],
            send_sem=edge_send.at[i], recv_sem=edge_recv.at[i],
            device_id={"strip": strip + 1 - 2 * i}, device_id_type=MESH,
        )
        for i in range(2)
    ]

    @pl.when(has_high)
    def _():
        edges[0].start()

    @pl.when(has_low)
    def _():
        edges[1].start()

    orders = [list(range(bits))]
    for t in range(1, tiles):
        orders.append([0] + list(range(2, bits)) + [1] if bits > 2 else orders[0])
    offsets = []
    for order in orders:
        offset = [jnp.int32(0)]
        for s, b in enumerate(order):
            offset.append(offset[-1] + ((me // (1 << b)) % 2) * (groups >> (s + 1)))
        offsets.append(offset)

    def partner(b):
        return me + (1 - 2 * ((me // (1 << b)) % 2)) * (1 << b)

    def halving(t, s):
        b = orders[t][s]
        half = groups >> (s + 1)
        away = offsets[t][s] + (1 - (me // (1 << b)) % 2) * half
        source = cand_ref if s == 0 else acc
        return pltpu.make_async_remote_copy(
            src_ref=source.at[t, pl.ds(away, half)],
            dst_ref=part_buf.at[t, pl.ds(groups - 2 * half, half)],
            send_sem=ref_send.at[t, s],
            recv_sem=ref_recv.at[t, s],
            device_id={"date": partner(b)},
            device_id_type=MESH,
        )

    def add_half(t, s):
        half = groups >> (s + 1)
        source = cand_ref if s == 0 else acc
        target = whole if s == bits - 1 else acc
        at = pl.ds(offsets[t][s + 1], half)
        target[t, at] = source[t, at] + part_buf[t, groups - 2 * half : groups - half]

    def doubling(t, s):
        half = groups >> (s + 1)
        mine = whole.at[t, pl.ds(offsets[t][s + 1], half)]
        return pltpu.make_async_remote_copy(
            src_ref=mine,
            dst_ref=mine,
            send_sem=ref_send.at[t, bits + s],
            recv_sem=ref_recv.at[t, bits + s],
            device_id={"date": partner(orders[t][s])},
            device_id_type=MESH,
        )

    state = {"step": 0, "copies": None}

    def advance():
        step = state["step"]
        if step > 2 * bits:
            return
        sent_now = []
        for t in range(tiles):
            if step > 0:
                state["copies"][t].wait()
                if step <= bits:
                    add_half(t, step - 1)
            if step < bits:
                sent_now.append(halving(t, step))
                sent_now[-1].start()
            elif step < 2 * bits:
                sent_now.append(doubling(t, 2 * bits - 1 - step))
                sent_now[-1].start()
        state["copies"] = sent_now
        state["step"] = step + 1

    lane = lax.broadcasted_iota(jnp.int32, (LANES, LANES), 1)
    window = 96

    def resample(d, t, first, last):
        def chip_line(a, carry):
            row0 = pl.multiple_of(a * CHIP_SIZE, CHIP_SIZE)
            q = (d * tiles + t) * 2
            for m in range((chips_rg + 1) // 2):
                span = slice(m * LANES, (m + 1) * LANES)
                halves = []
                mats = []
                for side, src in ((0, even_ref), (1, odd_ref)):
                    r = 2 * m + side
                    if r >= chips_rg:
                        continue
                    row_at = ((d * tiles + t) * chips_az + a) * chips_rg + r
                    line_row = lines_ref[pl.ds(row_at, 1), :]
                    col_row = cols_ref[pl.ds(row_at, 1), :]
                    line_mat = spread_rows(line_row, CHIP_SIZE).astype(bf16)[:, :window]
                    col_mat = spread_rows(col_row, LANES)
                    keep = lane < CHIP_SIZE if side == 0 else lane >= CHIP_SIZE
                    mats.append(jnp.where(keep, col_mat, 0.0).astype(bf16))
                    both = jnp.concatenate(
                        [src[q, pl.ds(row0, window), span], src[q + 1, pl.ds(row0, window), span]],
                        axis=1,
                    )
                    halves.append(
                        jnp.dot(line_mat, both, preferred_element_type=f32).astype(bf16)
                    )
                re = jnp.concatenate([h[:, :LANES] for h in halves], axis=1)
                im = jnp.concatenate([h[:, LANES:] for h in halves], axis=1)
                stacked = jnp.concatenate([re, im], axis=0)
                matrix = jnp.concatenate(mats, axis=0)
                out = jnp.dot(stacked, matrix, preferred_element_type=f32).astype(bf16)
                for c in range(2):
                    piece = out[c * CHIP_SIZE : (c + 1) * CHIP_SIZE]
                    series[d, t, c, m, pl.ds(row0, CHIP_SIZE), :] = piece.astype(f32)
                    if d == 0:
                        sent[t, c, m, pl.ds(row0, CHIP_SIZE), :] = piece
            return carry

        lax.fori_loop(first, last, chip_line, 0)

    advance()

    chip = 0
    for d in range(kept_dates):
        for t in range(tiles):
            for a in range(chips_az):
                for r in range(chips_rg):
                    values = (
                        shifts_ref[0, d, t, a, r] + (MARGIN - TAP_COUNT // 2 + 1),
                        (r % 2) * CHIP_SIZE
                        - shifts_ref[1, d, t, a, r]
                        - (MARGIN - TAP_COUNT // 2 + 1),
                        fractions_ref[0, d, t, a, r],
                        fractions_ref[1, d, t, a, r],
                    )
                    for i, value in enumerate(values):
                        spots[i, chip : chip + 1, :] = jnp.full((1, LANES), value, jnp.int32)
                    chip += 1
    at = lax.broadcasted_iota(jnp.int32, (chip, LANES), 1)
    lines_ref[:chip] = tap_weights(at - spots[0, :chip], spots[2, :chip])
    cols_ref[:chip] = tap_weights((spots[1, :chip] - at) & (LANES - 1), spots[3, :chip])

    @pl.when(has_low)
    def _():
        edges[0].wait_recv()

    @pl.when(has_high)
    def _():
        edges[1].wait_recv()

    @pl.when(strip == 0)
    def _():
        edge_in[0] = jnp.zeros(edge_in.shape[1:], bf16)

    @pl.when(strip == strips - 1)
    def _():
        edge_in[1] = jnp.zeros(edge_in.shape[1:], bf16)

    advance()
    tall = even_ref.shape[1]

    def picker(depth, width, want):
        source = lax.broadcasted_iota(jnp.int32, (depth, width), 0)
        at = lax.broadcasted_iota(jnp.int32, (depth, width), 1)
        return jnp.where(source == want(at), 1.0, 0.0).astype(bf16)

    def moved(values, matrix):
        return jnp.dot(values, matrix, preferred_element_type=f32).astype(bf16)

    both_move = picker(
        2 * LANES,
        2 * LANES,
        lambda at: jnp.where(at < LANES, at + LANES - MARGIN, at - LANES + CHIP_SIZE - MARGIN),
    )
    first_move = picker(LANES, LANES, lambda at: at - MARGIN)
    row_cut = (all_rows // 2 + 15) // 16 * 16

    def shift_image(q, carry):
        low_move = picker(LANES, LANES, lambda at: jnp.where(at < MARGIN, at + MARGIN * q, -1))
        skip = rest + MARGIN
        high_move = picker(
            LANES,
            LANES,
            lambda at: jnp.where(
                (at >= skip) & (at < skip + MARGIN), at - skip + MARGIN * q, -1
            ),
        )
        for row, size in ((0, row_cut), (row_cut, all_rows - row_cut)):
            span = slice(row, row + size)
            even_ref[q, span, :LANES] = moved(frame_ref[q, span, :LANES], first_move) + moved(
                edge_in[0, span, :], low_move
            )
            for m in range(blocks - 1):
                width = min(2 * LANES, cols - m * LANES)
                pair = moved(
                    frame_ref[q, span, m * LANES : m * LANES + width], both_move[:width]
                )
                block = pair[:, :LANES]
                if m == blocks - 2:
                    block = block + moved(edge_in[1, span, :], high_move)
                even_ref[q, span, (m + 1) * LANES : (m + 2) * LANES] = block
                odd_ref[q, span, m * LANES : (m + 1) * LANES] = pair[:, LANES:]
        even_ref[q, all_rows:, :] = jnp.zeros((tall - all_rows, wide), bf16)
        odd_ref[q, all_rows:, :] = jnp.zeros((tall - all_rows, odd_ref.shape[2]), bf16)
        return carry

    lax.fori_loop(0, images, shift_image, 0)
    last_d = series.shape[0] - 2
    following = [None]
    for d in range(last_d + 1):
        for t in range(tiles):
            advance()
            resample(d, t, 0, chips_az)
            if d == 0 and t == tiles - 1:
                following[0] = pltpu.make_async_remote_copy(
                    src_ref=sent, dst_ref=got, send_sem=next_send, recv_sem=next_recv,
                    device_id={"date": lax.rem(me + n - 1, n)}, device_id_type=MESH,
                )

                @pl.when(me > 0)
                def _():
                    following[0].start()

    @pl.when(me < n - 1)
    def _():
        following[0].wait_recv()

        def body(i, carry):
            row = pl.multiple_of(i * 16, 16)
            for t in range(tiles):
                for c in range(2):
                    for m in range(blocks):
                        series[last_d + 1, t, c, m, pl.ds(row, 16), :] = got[
                            t, c, m, pl.ds(row, 16), :
                        ].astype(f32)
            return carry

        lax.fori_loop(0, rows // 16, body, 0)

    @pl.when(me == n - 1)
    def _():
        series[last_d + 1] = jnp.zeros(series.shape[1:], f32)

    advance()
    dates = series.shape[0]
    pairs = dates - 1
    look_rows = rows // LOOK_AZ
    for t in range(tiles):
        def look_block(y, carry):
            def add(total, value):
                return value if total is None else total + value

            row = pl.multiple_of(y * GROUP, GROUP)
            for m in range(blocks):
                span = slice(m * LANES, (m + 1) * LANES)
                power = [None] * dates
                cross = [[None, None] for _ in range(pairs)]
                for s in range(LOOK_AZ):
                    lines_at = pl.ds(y * (GROUP * LOOK_AZ) + s, GROUP, stride=LOOK_AZ)
                    here = [
                        [series[d, t, c, m, lines_at, :] for c in range(2)] for d in range(dates)
                    ]
                    for d in range(dates):
                        re, im = here[d]
                        power[d] = add(power[d], re * re + im * im)
                    for p in range(pairs):
                        ar, ai = here[p]
                        br, bi = here[p + 1]
                        cross[p][0] = add(cross[p][0], ar * br + ai * bi)
                        cross[p][1] = add(cross[p][1], ai * br - ar * bi)
                for d in range(dates):
                    looks[t, d, pl.ds(row, GROUP), span] = power[d]
                for p in range(pairs):
                    for c in range(2):
                        looks[t, dates + 2 * p + c, pl.ds(row, GROUP), span] = cross[p][c]
            return carry

        lax.fori_loop(0, look_rows // GROUP, look_block, 0)
        advance()

    looks_rg = cols // LOOK_RG
    col_id = lax.broadcasted_iota(jnp.int32, (wide, LANES), 0)
    lane_id = lax.broadcasted_iota(jnp.int32, (wide, LANES), 1)
    base = col_id - LOOK_RG * lane_id

    def selector(q):
        shifted = base + LOOK_RG * looks_rg * q
        hit = (shifted >= 0) & (shifted < LOOK_RG) & (col_id < cols)
        return jnp.where(hit, 1.0, 0.0).astype(f32)

    numer = jnp.zeros((look_rows, LANES), f32)
    early = jnp.zeros((look_rows, LANES), f32)
    later = jnp.zeros((look_rows, LANES), f32)
    for p in range(pairs):
        for t in range(tiles):
            picks = [selector((c * pairs + p) * tiles + t) for c in range(2)]
            for c in range(2):
                numer = numer + split_dot(looks[t, dates + 2 * p + c], picks[c].astype(bf16))
            pick = (picks[0] + picks[1]).astype(bf16)
            early = early + split_dot(looks[t, p], pick)
            later = later + split_dot(looks[t, p + 1], pick)
    coherence = numer / jnp.sqrt((early + epsilon) * (later + epsilon))
    share = look_rows // n
    for j in range(n):
        out_buf[j] = coherence[j * share : (j + 1) * share]
    coh_ref[me] = out_buf[me]
    copies = []
    for o in range(1, n):
        peer = lax.rem(me + o, n)
        copy = pltpu.make_async_remote_copy(
            src_ref=out_buf.at[peer], dst_ref=coh_ref.at[me],
            send_sem=coh_send.at[o], recv_sem=coh_recv.at[o],
            device_id={"date": peer}, device_id_type=MESH,
        )
        copy.start()
        copies.append(copy)
    while state["step"] <= 2 * bits:
        advance()

    line_groups = CHIP_SIZE // GROUP
    kept = dates - 1
    for t in range(tiles):
        def corr_line(a, carry):
            for m in range(blocks):
                low = m * LANES
                size = min(LANES, cols - low)
                span = slice(low, low + size)
                total = [jnp.zeros((GROUP, size), f32)] * (1 + 3 * kept)
                for g in range(line_groups):
                    at = a * line_groups + g
                    rr = whole[t, at, :, span].astype(f32)
                    ri = whole[t, rows // GROUP + at, :, span].astype(f32)
                    total[0] = total[0] + (rr * rr + ri * ri)
                    row = pl.multiple_of(at * GROUP, GROUP)
                    for d in range(kept):
                        sr = series[d, t, 0, m, pl.ds(row, GROUP), :size]
                        si = series[d, t, 1, m, pl.ds(row, GROUP), :size]
                        total[1 + 3 * d] = total[1 + 3 * d] + (rr * sr + ri * si)
                        total[2 + 3 * d] = total[2 + 3 * d] + (ri * sr - rr * si)
                        total[3 + 3 * d] = total[3 + 3 * d] + (sr * sr + si * si)
                for k in range(1 + 3 * kept):
                    chip_rows[t, a, k : k + 1, span] = jnp.sum(total[k], axis=0, keepdims=True)
            return carry

        lax.fori_loop(0, chips_az, corr_line, 0)
    col_id = lax.broadcasted_iota(jnp.int32, (cols, LANES), 0)
    lane_id = lax.broadcasted_iota(jnp.int32, (cols, LANES), 1)
    gap = col_id - CHIP_SIZE * lane_id
    pick = jnp.where((gap >= 0) & (gap < CHIP_SIZE), 1.0, 0.0).astype(bf16)
    for t in range(tiles):
        for a in range(chips_az):
            sums_ref[t, a] = split_dot(chip_rows[t, a], pick)

    for o in range(1, n):
        copies[o - 1].wait()

    @pl.when(me > 0)
    def _():
        following[0].wait_send()

    @pl.when(has_high)
    def _():
        edges[0].wait_send()

    @pl.when(has_low)
    def _():
        edges[1].wait_send()


def per_device(n, strips, acquisitions, shifts, fractions, ref_dates):
    dates_local, tiles, _, all_rows, cols = acquisitions.shape
    rows = all_rows - 2 * MARGIN
    chips_az, chips_rg = shifts.shape[3:]
    blocks = -(-cols // LANES)
    wide = blocks * LANES
    images = dates_local * tiles * 2
    frames = acquisitions.reshape(images, all_rows, cols)
    tall = -(-all_rows // 32) * 32
    odd_wide = (chips_rg // 2) * LANES
    chips = dates_local * tiles * chips_az * chips_rg
    chips_tall = -(-chips // GROUP) * GROUP
    groups = -(-(2 * rows // GROUP) // n) * n

    look_rows = rows // LOOK_AZ
    looks_rg = cols // LOOK_RG
    share = look_rows // n
    stat_rows = 1 + 3 * dates_local
    bits = n.bit_length() - 1
    vmem = pl.BlockSpec(memory_space=pltpu.VMEM)
    f32 = jnp.float32
    bf16 = jnp.bfloat16
    dma = pltpu.SemaphoreType.DMA
    coh, sums = pl.pallas_call(
        functools.partial(kernel, n, strips, (tiles, chips_az, chips_rg, rows, cols)),
        out_shape=(
            jax.ShapeDtypeStruct((n, share, LANES), f32),
            jax.ShapeDtypeStruct((tiles, chips_az, stat_rows, LANES), f32),
        ),
        in_specs=[pl.BlockSpec(memory_space=pl.ANY)] + [pl.BlockSpec(memory_space=pltpu.SMEM)] * 3,
        out_specs=(vmem, vmem),
        scratch_shapes=[
            pltpu.VMEM((images, all_rows, cols), bf16),
            dma,
            pltpu.VMEM((images, tall, wide), bf16),
            pltpu.VMEM((images, tall, odd_wide), bf16),
            pltpu.VMEM((chips_tall, LANES), f32),
            pltpu.VMEM((chips_tall, LANES), f32),
            pltpu.VMEM((tiles, groups, GROUP, cols), bf16),
            pltpu.VMEM((2, all_rows, LANES), bf16),
            pltpu.VMEM((2, all_rows, LANES), bf16),
            pltpu.VMEM((all_rows, cols), f32),
            pltpu.VMEM((4, chips_tall, LANES), jnp.int32),
            pltpu.VMEM((dates_local + 1, tiles, 2, wide // LANES, rows, LANES), f32),
            pltpu.VMEM((tiles, 2, wide // LANES, rows, LANES), bf16),
            pltpu.VMEM((tiles, 2, wide // LANES, rows, LANES), bf16),
            pltpu.VMEM((tiles, groups, GROUP, cols), bf16),
            pltpu.VMEM((tiles, groups, GROUP, cols), bf16),
            pltpu.VMEM((tiles, groups, GROUP, cols), bf16),
            pltpu.VMEM((tiles, dates_local + 1 + 2 * dates_local, look_rows, wide), f32),
            pltpu.VMEM((tiles, chips_az, stat_rows, cols), f32),
            pltpu.VMEM((n, share, LANES), f32),
            dma((tiles, 2 * bits)), dma((tiles, 2 * bits)), dma, dma, dma((n,)), dma((n,)),
            dma((2,)), dma((2,)),
        ],
        compiler_params=pltpu.CompilerParams(
            collective_id=0, has_side_effects=True, vmem_limit_bytes=50 * 1024 * 1024
        ),
    )(frames, shifts, fractions, ref_dates)

    stats = sums[..., :chips_rg]
    ref_power = stats[:, :, 0]
    sec = stats[:, :, 1:].reshape(tiles, chips_az, dates_local, 3, chips_rg)
    sec = sec.transpose(3, 2, 0, 1, 4)
    denominator = jnp.sqrt((ref_power[None] + epsilon) * (sec[2] + epsilon))
    chip_corr = sec[:2] / denominator[None]
    looked = coh.reshape(n, share, 2, dates_local, tiles, looks_rg)
    looked = looked.transpose(2, 0, 3, 4, 1, 5).reshape(2, n * dates_local, tiles, share, looks_rg)
    return (chip_corr, looked[:, : n * dates_local - 1])


def solution(mesh):
    return jax.shard_map(
        functools.partial(per_device, mesh.shape["date"], mesh.shape["strip"]),
        mesh=mesh,
        in_specs=(
            P("date", None, None, None, "strip"),
            P(None, "date", None, None, "strip"),
            P(None, "date", None, None, "strip"),
            P(),
        ),
        out_specs=(P(None, "date", None, None, "strip"), P(None, None, None, "date", "strip")),
        check_vma=False,
    )
```

```python
import functools

import jax
import jax.numpy as jnp
from jax import lax
from jax.experimental import pallas as pl
from jax.experimental.pallas import tpu as pltpu
from jax.sharding import PartitionSpec as P

TILE_COUNT = 2
CHIP_SIZE = 64
TAP_COUNT = 8
SUBSTEPS = 64
LOOK_AZ = 5
LOOK_RG = 20
MARGIN = 12
LANES = 128
GROUP = 8

epsilon = 1e-06
MESH = pl.DeviceIdType.MESH


def tap_weights(k, fraction):
    distance = k.astype(jnp.float32) - (TAP_COUNT // 2 - 1) - fraction.astype(jnp.float32) / SUBSTEPS
    angle = jnp.pi * distance
    sinc = jnp.where(
        distance == 0.0, 1.0, jnp.sin(angle) / jnp.where(distance == 0.0, 1.0, angle)
    )
    weights = sinc * (0.5 + 0.5 * jnp.cos(jnp.pi * distance / (TAP_COUNT // 2)))
    weights = jnp.where((k >= 0) & (k < TAP_COUNT), weights, 0.0)
    return weights / jnp.sum(weights, axis=1, keepdims=True)


def spread_rows(row, count):
    tall = jnp.broadcast_to(row, (count, LANES))
    return pltpu.roll(tall, 0, 1, stride=1, stride_axis=0)


def split_dot(values, selector):
    high = values.astype(jnp.bfloat16)
    low = (values - high.astype(jnp.float32)).astype(jnp.bfloat16)
    return jnp.dot(high, selector, preferred_element_type=jnp.float32) + jnp.dot(
        low, selector, preferred_element_type=jnp.float32
    )


def kernel(
    n, strips, dims,
    frame_hbm, shifts_ref, fractions_ref, dates_ref,
    coh_ref, sums_ref,
    frame_ref, frame_sem, even_ref, odd_ref, lines_ref, cols_ref, cand_ref, edge_out, edge_in, picked, spots,
    series, sent, got, acc, part_buf, whole, looks, chip_rows, out_buf,
    ref_send, ref_recv, next_send, next_recv, coh_send, coh_recv, edge_send, edge_recv,
):
    tiles, chips_az, chips_rg, rows, cols = dims
    me = lax.axis_index("date")
    strip = lax.axis_index("strip")
    bits = n.bit_length() - 1
    groups = cand_ref.shape[1]
    all_rows = rows + 2 * MARGIN
    blocks = series.shape[3]
    wide = blocks * LANES
    kept_dates = series.shape[0] - 1
    images = frame_ref.shape[0]
    rest = cols - (blocks - 1) * LANES
    bf16 = jnp.bfloat16
    f32 = jnp.float32

    load = pltpu.make_async_copy(frame_hbm, frame_ref, frame_sem)
    load.start()
    barrier = pltpu.get_barrier_semaphore()
    for o in range(1, n):
        pl.semaphore_signal(
            barrier, inc=1, device_id={"date": lax.rem(me + o, n)}, device_id_type=MESH
        )
    has_low = strip > 0
    has_high = strip < strips - 1

    @pl.when(has_low)
    def _():
        pl.semaphore_signal(barrier, inc=1, device_id={"strip": strip - 1}, device_id_type=MESH)

    @pl.when(has_high)
    def _():
        pl.semaphore_signal(barrier, inc=1, device_id={"strip": strip + 1}, device_id_type=MESH)

    def for_rows(body):
        count = all_rows // CHIP_SIZE

        def step(i, carry):
            body(pl.multiple_of(i * CHIP_SIZE, CHIP_SIZE), CHIP_SIZE)
            return carry

        lax.fori_loop(0, count, step, 0)
        if all_rows > count * CHIP_SIZE:
            body(count * CHIP_SIZE, all_rows - count * CHIP_SIZE)

    def block_of(q, row, size, m):
        width = min(LANES, cols - m * LANES)
        value = frame_ref[q, pl.ds(row, size), m * LANES : m * LANES + width].astype(f32)
        if width < LANES:
            value = jnp.concatenate([value, jnp.zeros((size, LANES - width), f32)], axis=1)
        return value

    def pack_edges(row, size):
        at = lax.broadcasted_iota(jnp.int32, (size, LANES), 1)
        right = jnp.zeros((size, LANES), f32)
        left = jnp.zeros((size, LANES), f32)
        for q in range(images):
            place = (at >= MARGIN * q) & (at < MARGIN * (q + 1))
            last = block_of(q, row, size, blocks - 1)
            first = block_of(q, row, size, 0)
            last = pltpu.roll(last, (MARGIN * q - rest + MARGIN) % LANES, 1)
            if q:
                first = pltpu.roll(first, MARGIN * q, 1)
            right = jnp.where(place, last, right)
            left = jnp.where(place, first, left)
        edge_out[0, pl.ds(row, size), :] = right.astype(bf16)
        edge_out[1, pl.ds(row, size), :] = left.astype(bf16)

    load.wait()
    for_rows(pack_edges)

    def pick_tile(tc, carry):
        t = tc // 2
        gains = [
            jnp.where(dates_ref[t] == me * kept_dates + d, 1.0, 0.0).astype(f32)
            for d in range(kept_dates)
        ]

        def select(row, size):
            total = jnp.zeros((size, cols), f32)
            for d in range(kept_dates):
                image = frame_ref[d * tiles * 2 + tc, pl.ds(row, size), :]
                total = total + image.astype(f32) * gains[d]
            picked[pl.ds(row, size), :] = total

        for_rows(select)
        count = rows // GROUP
        for g in range(count):
            low = MARGIN + g * GROUP
            cand_ref[t, (tc % 2) * count + g] = picked[low : low + GROUP, :].astype(bf16)
        return carry

    lax.fori_loop(0, tiles * 2, pick_tile, 0)

    beside = jnp.minimum(strip, 1) + jnp.minimum(strips - 1 - strip, 1)
    pl.semaphore_wait(barrier, n - 1 + beside)

    edges = [
        pltpu.make_async_remote_copy(
            src_ref=edge_out.at[i], dst_ref=edge_in.at[i],
            send_sem=edge_send.at[i], recv_sem=edge_recv.at[i],
            device_id={"strip": strip + 1 - 2 * i}, device_id_type=MESH,
        )
        for i in range(2)
    ]

    @pl.when(has_high)
    def _():
        edges[0].start()

    @pl.when(has_low)
    def _():
        edges[1].start()

    orders = [list(range(bits))]
    for t in range(1, tiles):
        orders.append([0] + list(range(2, bits)) + [1] if bits > 2 else orders[0])
    offsets = []
    for order in orders:
        offset = [jnp.int32(0)]
        for s, b in enumerate(order):
            offset.append(offset[-1] + ((me // (1 << b)) % 2) * (groups >> (s + 1)))
        offsets.append(offset)

    def partner(b):
        return me + (1 - 2 * ((me // (1 << b)) % 2)) * (1 << b)

    def halving(t, s):
        b = orders[t][s]
        half = groups >> (s + 1)
        away = offsets[t][s] + (1 - (me // (1 << b)) % 2) * half
        source = cand_ref if s == 0 else acc
        return pltpu.make_async_remote_copy(
            src_ref=source.at[t, pl.ds(away, half)],
            dst_ref=part_buf.at[t, pl.ds(groups - 2 * half, half)],
            send_sem=ref_send.at[t, s],
            recv_sem=ref_recv.at[t, s],
            device_id={"date": partner(b)},
            device_id_type=MESH,
        )

    def add_half(t, s):
        half = groups >> (s + 1)
        source = cand_ref if s == 0 else acc
        target = whole if s == bits - 1 else acc
        at = pl.ds(offsets[t][s + 1], half)
        target[t, at] = source[t, at] + part_buf[t, groups - 2 * half : groups - half]

    def doubling(t, s):
        half = groups >> (s + 1)
        mine = whole.at[t, pl.ds(offsets[t][s + 1], half)]
        return pltpu.make_async_remote_copy(
            src_ref=mine,
            dst_ref=mine,
            send_sem=ref_send.at[t, bits + s],
            recv_sem=ref_recv.at[t, bits + s],
            device_id={"date": partner(orders[t][s])},
            device_id_type=MESH,
        )

    state = {"step": 0, "copies": None}

    def advance():
        step = state["step"]
        if step > 2 * bits:
            return
        sent_now = []
        for t in range(tiles):
            if step > 0:
                state["copies"][t].wait()
                if step <= bits:
                    add_half(t, step - 1)
            if step < bits:
                sent_now.append(halving(t, step))
                sent_now[-1].start()
            elif step < 2 * bits:
                sent_now.append(doubling(t, 2 * bits - 1 - step))
                sent_now[-1].start()
        state["copies"] = sent_now
        state["step"] = step + 1

    lane = lax.broadcasted_iota(jnp.int32, (LANES, LANES), 1)
    window = 96

    def resample(d, t, first, last):
        def chip_line(a, carry):
            row0 = pl.multiple_of(a * CHIP_SIZE, CHIP_SIZE)
            q = (d * tiles + t) * 2
            for m in range((chips_rg + 1) // 2):
                span = slice(m * LANES, (m + 1) * LANES)
                halves = []
                mats = []
                for side, src in ((0, even_ref), (1, odd_ref)):
                    r = 2 * m + side
                    if r >= chips_rg:
                        continue
                    row_at = ((d * tiles + t) * chips_az + a) * chips_rg + r
                    line_row = lines_ref[pl.ds(row_at, 1), :]
                    col_row = cols_ref[pl.ds(row_at, 1), :]
                    line_mat = spread_rows(line_row, CHIP_SIZE).astype(bf16)[:, :window]
                    col_mat = spread_rows(col_row, LANES)
                    keep = lane < CHIP_SIZE if side == 0 else lane >= CHIP_SIZE
                    mats.append(jnp.where(keep, col_mat, 0.0).astype(bf16))
                    both = jnp.concatenate(
                        [src[q, pl.ds(row0, window), span], src[q + 1, pl.ds(row0, window), span]],
                        axis=1,
                    )
                    halves.append(
                        jnp.dot(line_mat, both, preferred_element_type=f32).astype(bf16)
                    )
                re = jnp.concatenate([h[:, :LANES] for h in halves], axis=1)
                im = jnp.concatenate([h[:, LANES:] for h in halves], axis=1)
                stacked = jnp.concatenate([re, im], axis=0)
                matrix = jnp.concatenate(mats, axis=0)
                out = jnp.dot(stacked, matrix, preferred_element_type=f32).astype(bf16)
                for c in range(2):
                    piece = out[c * CHIP_SIZE : (c + 1) * CHIP_SIZE]
                    series[d, t, c, m, pl.ds(row0, CHIP_SIZE), :] = piece.astype(f32)
                    if d == 0:
                        sent[t, c, m, pl.ds(row0, CHIP_SIZE), :] = piece
            return carry

        lax.fori_loop(first, last, chip_line, 0)

    advance()

    chip = 0
    for d in range(kept_dates):
        for t in range(tiles):
            for a in range(chips_az):
                for r in range(chips_rg):
                    values = (
                        shifts_ref[0, d, t, a, r] + (MARGIN - TAP_COUNT // 2 + 1),
                        (r % 2) * CHIP_SIZE
                        - shifts_ref[1, d, t, a, r]
                        - (MARGIN - TAP_COUNT // 2 + 1),
                        fractions_ref[0, d, t, a, r],
                        fractions_ref[1, d, t, a, r],
                    )
                    for i, value in enumerate(values):
                        spots[i, chip : chip + 1, :] = jnp.full((1, LANES), value, jnp.int32)
                    chip += 1
    at = lax.broadcasted_iota(jnp.int32, (chip, LANES), 1)
    lines_ref[:chip] = tap_weights(at - spots[0, :chip], spots[2, :chip])
    cols_ref[:chip] = tap_weights((spots[1, :chip] - at) & (LANES - 1), spots[3, :chip])

    @pl.when(has_low)
    def _():
        edges[0].wait_recv()

    @pl.when(has_high)
    def _():
        edges[1].wait_recv()

    @pl.when(strip == 0)
    def _():
        edge_in[0] = jnp.zeros(edge_in.shape[1:], bf16)

    @pl.when(strip == strips - 1)
    def _():
        edge_in[1] = jnp.zeros(edge_in.shape[1:], bf16)

    advance()
    tall = even_ref.shape[1]

    def picker(depth, width, want):
        source = lax.broadcasted_iota(jnp.int32, (depth, width), 0)
        at = lax.broadcasted_iota(jnp.int32, (depth, width), 1)
        return jnp.where(source == want(at), 1.0, 0.0).astype(bf16)

    def moved(values, matrix):
        return jnp.dot(values, matrix, preferred_element_type=f32).astype(bf16)

    both_move = picker(
        2 * LANES,
        2 * LANES,
        lambda at: jnp.where(at < LANES, at + LANES - MARGIN, at - LANES + CHIP_SIZE - MARGIN),
    )
    first_move = picker(LANES, LANES, lambda at: at - MARGIN)
    row_cut = (all_rows // 2 + 15) // 16 * 16

    def shift_image(q, carry):
        low_move = picker(LANES, LANES, lambda at: jnp.where(at < MARGIN, at + MARGIN * q, -1))
        skip = rest + MARGIN
        high_move = picker(
            LANES,
            LANES,
            lambda at: jnp.where(
                (at >= skip) & (at < skip + MARGIN), at - skip + MARGIN * q, -1
            ),
        )
        for row, size in ((0, row_cut), (row_cut, all_rows - row_cut)):
            span = slice(row, row + size)
            even_ref[q, span, :LANES] = moved(frame_ref[q, span, :LANES], first_move) + moved(
                edge_in[0, span, :], low_move
            )
            for m in range(blocks - 1):
                width = min(2 * LANES, cols - m * LANES)
                pair = moved(
                    frame_ref[q, span, m * LANES : m * LANES + width], both_move[:width]
                )
                block = pair[:, :LANES]
                if m == blocks - 2:
                    block = block + moved(edge_in[1, span, :], high_move)
                even_ref[q, span, (m + 1) * LANES : (m + 2) * LANES] = block
                odd_ref[q, span, m * LANES : (m + 1) * LANES] = pair[:, LANES:]
        even_ref[q, all_rows:, :] = jnp.zeros((tall - all_rows, wide), bf16)
        odd_ref[q, all_rows:, :] = jnp.zeros((tall - all_rows, odd_ref.shape[2]), bf16)
        return carry

    lax.fori_loop(0, images, shift_image, 0)
    last_d = series.shape[0] - 2
    following = [None]
    for d in range(last_d + 1):
        for t in range(tiles):
            advance()
            resample(d, t, 0, chips_az)
            if d == 0 and t == tiles - 1:
                following[0] = pltpu.make_async_remote_copy(
                    src_ref=sent, dst_ref=got, send_sem=next_send, recv_sem=next_recv,
                    device_id={"date": lax.rem(me + n - 1, n)}, device_id_type=MESH,
                )

                @pl.when(me > 0)
                def _():
                    following[0].start()

    advance()

    @pl.when(me < n - 1)
    def _():
        following[0].wait_recv()

        def body(i, carry):
            row = pl.multiple_of(i * 16, 16)
            for t in range(tiles):
                for c in range(2):
                    for m in range(blocks):
                        series[last_d + 1, t, c, m, pl.ds(row, 16), :] = got[
                            t, c, m, pl.ds(row, 16), :
                        ].astype(f32)
            return carry

        lax.fori_loop(0, rows // 16, body, 0)

    @pl.when(me == n - 1)
    def _():
        series[last_d + 1] = jnp.zeros(series.shape[1:], f32)

    advance()
    dates = series.shape[0]
    pairs = dates - 1
    look_rows = rows // LOOK_AZ
    for t in range(tiles):
        def look_block(y, carry):
            def add(total, value):
                return value if total is None else total + value

            row = pl.multiple_of(y * GROUP, GROUP)
            for m in range(blocks):
                span = slice(m * LANES, (m + 1) * LANES)
                power = [None] * dates
                cross = [[None, None] for _ in range(pairs)]
                for s in range(LOOK_AZ):
                    lines_at = pl.ds(y * (GROUP * LOOK_AZ) + s, GROUP, stride=LOOK_AZ)
                    here = [
                        [series[d, t, c, m, lines_at, :] for c in range(2)] for d in range(dates)
                    ]
                    for d in range(dates):
                        re, im = here[d]
                        power[d] = add(power[d], re * re + im * im)
                    for p in range(pairs):
                        ar, ai = here[p]
                        br, bi = here[p + 1]
                        cross[p][0] = add(cross[p][0], ar * br + ai * bi)
                        cross[p][1] = add(cross[p][1], ai * br - ar * bi)
                for d in range(dates):
                    looks[t, d, pl.ds(row, GROUP), span] = power[d]
                for p in range(pairs):
                    for c in range(2):
                        looks[t, dates + 2 * p + c, pl.ds(row, GROUP), span] = cross[p][c]
            return carry

        lax.fori_loop(0, look_rows // GROUP, look_block, 0)
        advance()

    looks_rg = cols // LOOK_RG
    col_id = lax.broadcasted_iota(jnp.int32, (wide, LANES), 0)
    lane_id = lax.broadcasted_iota(jnp.int32, (wide, LANES), 1)
    base = col_id - LOOK_RG * lane_id

    def selector(q):
        shifted = base + LOOK_RG * looks_rg * q
        hit = (shifted >= 0) & (shifted < LOOK_RG) & (col_id < cols)
        return jnp.where(hit, 1.0, 0.0).astype(f32)

    numer = jnp.zeros((look_rows, LANES), f32)
    early = jnp.zeros((look_rows, LANES), f32)
    later = jnp.zeros((look_rows, LANES), f32)
    for p in range(pairs):
        for t in range(tiles):
            picks = [selector((c * pairs + p) * tiles + t) for c in range(2)]
            for c in range(2):
                numer = numer + split_dot(looks[t, dates + 2 * p + c], picks[c].astype(bf16))
            pick = (picks[0] + picks[1]).astype(bf16)
            early = early + split_dot(looks[t, p], pick)
            later = later + split_dot(looks[t, p + 1], pick)
    coherence = numer / jnp.sqrt((early + epsilon) * (later + epsilon))
    share = look_rows // n
    for j in range(n):
        out_buf[j] = coherence[j * share : (j + 1) * share]
    coh_ref[me] = out_buf[me]
    copies = []
    for o in range(1, n):
        peer = lax.rem(me + o, n)
        copy = pltpu.make_async_remote_copy(
            src_ref=out_buf.at[peer], dst_ref=coh_ref.at[me],
            send_sem=coh_send.at[o], recv_sem=coh_recv.at[o],
            device_id={"date": peer}, device_id_type=MESH,
        )
        copy.start()
        copies.append(copy)
    while state["step"] <= 2 * bits:
        advance()

    line_groups = CHIP_SIZE // GROUP
    kept = dates - 1
    for t in range(tiles):
        def corr_line(a, carry):
            for m in range(blocks):
                low = m * LANES
                size = min(LANES, cols - low)
                span = slice(low, low + size)
                total = [jnp.zeros((GROUP, size), f32)] * (1 + 3 * kept)
                for g in range(line_groups):
                    at = a * line_groups + g
                    rr = whole[t, at, :, span].astype(f32)
                    ri = whole[t, rows // GROUP + at, :, span].astype(f32)
                    total[0] = total[0] + (rr * rr + ri * ri)
                    row = pl.multiple_of(at * GROUP, GROUP)
                    for d in range(kept):
                        sr = series[d, t, 0, m, pl.ds(row, GROUP), :size]
                        si = series[d, t, 1, m, pl.ds(row, GROUP), :size]
                        total[1 + 3 * d] = total[1 + 3 * d] + (rr * sr + ri * si)
                        total[2 + 3 * d] = total[2 + 3 * d] + (ri * sr - rr * si)
                        total[3 + 3 * d] = total[3 + 3 * d] + (sr * sr + si * si)
                for k in range(1 + 3 * kept):
                    chip_rows[t, a, k : k + 1, span] = jnp.sum(total[k], axis=0, keepdims=True)
            return carry

        lax.fori_loop(0, chips_az, corr_line, 0)
    col_id = lax.broadcasted_iota(jnp.int32, (cols, LANES), 0)
    lane_id = lax.broadcasted_iota(jnp.int32, (cols, LANES), 1)
    gap = col_id - CHIP_SIZE * lane_id
    pick = jnp.where((gap >= 0) & (gap < CHIP_SIZE), 1.0, 0.0).astype(bf16)
    for t in range(tiles):
        for a in range(chips_az):
            sums_ref[t, a] = split_dot(chip_rows[t, a], pick)

    for o in range(1, n):
        copies[o - 1].wait()

    @pl.when(me > 0)
    def _():
        following[0].wait_send()

    @pl.when(has_high)
    def _():
        edges[0].wait_send()

    @pl.when(has_low)
    def _():
        edges[1].wait_send()


def per_device(n, strips, acquisitions, shifts, fractions, ref_dates):
    dates_local, tiles, _, all_rows, cols = acquisitions.shape
    rows = all_rows - 2 * MARGIN
    chips_az, chips_rg = shifts.shape[3:]
    blocks = -(-cols // LANES)
    wide = blocks * LANES
    images = dates_local * tiles * 2
    frames = acquisitions.reshape(images, all_rows, cols)
    tall = -(-all_rows // 32) * 32
    odd_wide = (chips_rg // 2) * LANES
    chips = dates_local * tiles * chips_az * chips_rg
    chips_tall = -(-chips // GROUP) * GROUP
    groups = -(-(2 * rows // GROUP) // n) * n

    look_rows = rows // LOOK_AZ
    looks_rg = cols // LOOK_RG
    share = look_rows // n
    stat_rows = 1 + 3 * dates_local
    bits = n.bit_length() - 1
    vmem = pl.BlockSpec(memory_space=pltpu.VMEM)
    f32 = jnp.float32
    bf16 = jnp.bfloat16
    dma = pltpu.SemaphoreType.DMA
    coh, sums = pl.pallas_call(
        functools.partial(kernel, n, strips, (tiles, chips_az, chips_rg, rows, cols)),
        out_shape=(
            jax.ShapeDtypeStruct((n, share, LANES), f32),
            jax.ShapeDtypeStruct((tiles, chips_az, stat_rows, LANES), f32),
        ),
        in_specs=[pl.BlockSpec(memory_space=pl.ANY)] + [pl.BlockSpec(memory_space=pltpu.SMEM)] * 3,
        out_specs=(vmem, vmem),
        scratch_shapes=[
            pltpu.VMEM((images, all_rows, cols), bf16),
            dma,
            pltpu.VMEM((images, tall, wide), bf16),
            pltpu.VMEM((images, tall, odd_wide), bf16),
            pltpu.VMEM((chips_tall, LANES), f32),
            pltpu.VMEM((chips_tall, LANES), f32),
            pltpu.VMEM((tiles, groups, GROUP, cols), bf16),
            pltpu.VMEM((2, all_rows, LANES), bf16),
            pltpu.VMEM((2, all_rows, LANES), bf16),
            pltpu.VMEM((all_rows, cols), f32),
            pltpu.VMEM((4, chips_tall, LANES), jnp.int32),
            pltpu.VMEM((dates_local + 1, tiles, 2, wide // LANES, rows, LANES), f32),
            pltpu.VMEM((tiles, 2, wide // LANES, rows, LANES), bf16),
            pltpu.VMEM((tiles, 2, wide // LANES, rows, LANES), bf16),
            pltpu.VMEM((tiles, groups, GROUP, cols), bf16),
            pltpu.VMEM((tiles, groups, GROUP, cols), bf16),
            pltpu.VMEM((tiles, groups, GROUP, cols), bf16),
            pltpu.VMEM((tiles, dates_local + 1 + 2 * dates_local, look_rows, wide), f32),
            pltpu.VMEM((tiles, chips_az, stat_rows, cols), f32),
            pltpu.VMEM((n, share, LANES), f32),
            dma((tiles, 2 * bits)), dma((tiles, 2 * bits)), dma, dma, dma((n,)), dma((n,)),
            dma((2,)), dma((2,)),
        ],
        compiler_params=pltpu.CompilerParams(
            collective_id=0, has_side_effects=True, vmem_limit_bytes=50 * 1024 * 1024
        ),
    )(frames, shifts, fractions, ref_dates)

    stats = sums[..., :chips_rg]
    ref_power = stats[:, :, 0]
    sec = stats[:, :, 1:].reshape(tiles, chips_az, dates_local, 3, chips_rg)
    sec = sec.transpose(3, 2, 0, 1, 4)
    denominator = jnp.sqrt((ref_power[None] + epsilon) * (sec[2] + epsilon))
    chip_corr = sec[:2] / denominator[None]
    looked = coh.reshape(n, share, 2, dates_local, tiles, looks_rg)
    looked = looked.transpose(2, 0, 3, 4, 1, 5).reshape(2, n * dates_local, tiles, share, looks_rg)
    return (chip_corr, looked[:, : n * dates_local - 1])


def solution(mesh):
    return jax.shard_map(
        functools.partial(per_device, mesh.shape["date"], mesh.shape["strip"]),
        mesh=mesh,
        in_specs=(
            P("date", None, None, None, "strip"),
            P(None, "date", None, None, "strip"),
            P(None, "date", None, None, "strip"),
            P(),
        ),
        out_specs=(P(None, "date", None, None, "strip"), P(None, None, None, "date", "strip")),
        check_vma=False,
    )
```
